512 devices in a mesh: chan: 64 (over y, z_lo, core), lag: 4 (over x), seg: 2 (over z_hi).
Axes of the slice: x: 4, y: 4, z: 16 (z_hi: 2, z_lo: 8; z = z_hi * 8 + z_lo), core: 2. Of those that a mesh axis runs over, the one named last changes fastest.
Arguments:
- records_owned: float32 [8192, 2, 1024], P('chan', 'seg', 'lag'), may hold values from -6 to 6
- section_list: int32 [8192], replicated, may hold values from 0 to 8191, as said below
- ref_index: int32 [64], replicated, may hold values from 0 to 8191, as said below
Outputs:
- correlations: float32 [8192, 8192], P(('chan', 'seg'), 'lag')
The draws below stay inside these ranges and needn't reach their ends.
Inputs may be any that keep to these rules, and one draw needn't show every extreme that they name: `section_list`: each value names a channel once. The 128 rows of each owner name exactly 2 channels of every channel block (channels b*128 to (b+1)*128 - 1). `ref_index`: distinct channel numbers.
All inputs are finite; a program needn't handle non-finite values.
Results may differ from the reference program's by a relative error of at most 0.000098.
Values sent between devices are 32-bit elements; how exact they have to be, the bound alone decides.
A program may use at most 64 MiB of HBM per device.

```python
import math
import jax
import jax.numpy as jnp
from jax import lax

CH_DEV = 128
REF = 64
LAGS = 128
SAMPLES = 2048
CHANNELS = 8192
SEGS = 2
SEG_LEN = 1024
NTERMS = 1920


def draw_section_list(key, part):
    blocks = CHANNELS // CH_DEV
    peers = CH_DEV // blocks
    first_key, second_key = jax.random.split(jax.random.fold_in(key, 11))
    positions = jnp.arange(CH_DEV, dtype=jnp.int32)[None, :]
    scores = jax.random.randint(first_key, (blocks, CH_DEV), 0, 1 << 16) * CH_DEV + positions
    ordering = jnp.argsort(scores, axis=1).astype(jnp.int32)
    channel_ids = ordering + (jnp.arange(blocks, dtype=jnp.int32) * CH_DEV)[:, None]
    channel_ids = channel_ids.reshape(blocks, blocks, peers).transpose(1, 0, 2).reshape(blocks, CH_DEV)
    mixing = jax.random.randint(second_key, (blocks, CH_DEV), 0, 1 << 16) * CH_DEV + positions
    shuffle = jnp.argsort(mixing, axis=1).astype(jnp.int32)
    channel_ids = jnp.take_along_axis(channel_ids, shuffle, axis=1)
    return channel_ids.reshape(CHANNELS).astype(jnp.int32)


def draw_ref_index(key, part):
    chosen = jax.random.permutation(jax.random.fold_in(key, 23), CHANNELS)
    return chosen[:REF].astype(jnp.int32)


def steps_of(own_key, dims, cuts, least, largest):
    factor_of, own = 1.0, jax.random.fold_in(own_key, 6)
    for position, blocks in cuts:
        draws = jnp.exp(jax.random.uniform(jax.random.fold_in(own, position), (blocks,), jnp.float32, least / len(cuts), largest / len(cuts)))
        factor_of = factor_of * jnp.repeat(draws, dims[position] // blocks).reshape([-1 if axis == position else 1 for axis in range(len(dims))])
    return factor_of


def centred(stream_key, extent, deviation, limit, pieces=(), held_as=jnp.bfloat16):
    level = steps_of(stream_key, extent, pieces, -0.22, 0.18) if pieces else 1.0
    values = jax.random.normal(stream_key, extent, jnp.float32) * deviation * level
    return jnp.minimum(jnp.maximum(values, -limit), limit).astype(held_as)


def setup_inputs(seed: int = 0) -> dict:
    arg_keys = jax.random.split(jax.random.key(seed), 4)
    records_owned = centred(arg_keys[0], (CHANNELS, SEGS, SEG_LEN), 1.0, 6.0, ((0, 64), (1, 2), (2, 4)), jnp.float32)
    section_list = draw_section_list(jax.random.fold_in(arg_keys[3], 71), 0)
    ref_index = draw_ref_index(jax.random.fold_in(arg_keys[3], 71), 0)
    return dict(records_owned=records_owned, section_list=section_list, ref_index=ref_index)


def reference(records_owned, section_list, ref_index):
    flat = records_owned.reshape(CHANNELS, SAMPLES)
    series = flat[jnp.argsort(section_list).astype(jnp.int32)]
    panel = series[ref_index][:, :NTERMS]

    def one_lag(lag_value):
        window = lax.dynamic_slice_in_dim(series, lag_value, NTERMS, 1)
        return jnp.dot(window, panel.T, precision=lax.Precision.HIGHEST, preferred_element_type=jnp.float32)
    stacked = lax.map(one_lag, jnp.arange(LAGS, dtype=jnp.int32))
    result = jnp.transpose(stacked, (1, 0, 2)).reshape(CHANNELS, LAGS * REF)
    return result / math.sqrt(NTERMS)
```

```python
import math

import jax
import jax.numpy as jnp
from jax import lax
from jax.experimental import pallas as pl
from jax.experimental.pallas import tpu as pltpu
from jax.sharding import PartitionSpec as P

LAGS = 128
SAMPLES = 2048
REF = 64
TERMS = SAMPLES - LAGS
LANES = 128
TILES = SAMPLES // LANES
COLUMN_LAGS = 4


def split(value):
    high = value.astype(jnp.bfloat16)
    return high, (value - high.astype(jnp.float32)).astype(jnp.bfloat16)


def transposed_dot(left, right):
    return lax.dot_general(
        left, right, (((1,), (1,)), ((), ())), preferred_element_type=jnp.float32
    )


def correlate(series_ref, panel_ref, out_ref, windows_high, windows_low, shifts_high, shifts_low):
    lag_width = LAGS // lax.axis_size("lag")
    rows = series_ref.shape[1]
    groups = lag_width // COLUMN_LAGS
    start = lax.axis_index("lag") * lag_width
    panel = jnp.concatenate(
        [panel_ref[tile] for tile in range(TERMS // LANES)]
        + [jnp.zeros((REF, LANES), jnp.float32)] * (TILES - TERMS // LANES),
        axis=1,
    )
    panel = pltpu.roll(panel, start, 1)
    for shift in range(COLUMN_LAGS):
        high, low = split(pltpu.roll(panel, shift, 1) if shift else panel)
        shifts_high[pl.ds(shift * REF, REF), :] = high
        shifts_low[pl.ds(shift * REF, REF), :] = low
    series = jnp.concatenate([series_ref[tile] for tile in range(TILES)], axis=1)
    for group in range(groups):
        lag = group * COLUMN_LAGS
        high, low = split(pltpu.roll(series, SAMPLES - lag, 1) if lag else series)
        windows_high[pl.ds(group * rows, rows), :] = high
        windows_low[pl.ds(group * rows, rows), :] = low
    total = (
        transposed_dot(windows_high[...], shifts_high[...])
        + transposed_dot(windows_high[...], shifts_low[...])
        + transposed_dot(windows_low[...], shifts_high[...])
    )
    width = COLUMN_LAGS * REF
    for group in range(groups):
        out_ref[:, pl.ds(group * width, width)] = total[group * rows : (group + 1) * rows] * (
            1.0 / math.sqrt(TERMS)
        )


def select_rows(one_hot, values):
    return jnp.dot(
        one_hot.astype(jnp.float32),
        values,
        precision=lax.Precision.HIGHEST,
        preferred_element_type=jnp.float32,
    )


def shards(records_owned, section_list, ref_index):
    blocks = lax.axis_size("chan")
    own_block = lax.axis_index("chan")
    segment = lax.axis_index("seg")
    block_rows = records_owned.shape[0]
    half_rows = block_rows // lax.axis_size("seg")
    samples = records_owned.shape[2]
    owner_lists = section_list.reshape(blocks, block_rows)
    own_list = lax.dynamic_slice_in_dim(owner_lists, own_block, 1, 0)[0]
    list_block = own_list // block_rows
    behind = (list_block[:, None] == list_block[None, :]) & (own_list[:, None] < own_list[None, :])
    rank = jnp.sum(behind.astype(jnp.int32), axis=0)
    wanted = jnp.arange(blocks)
    chosen = jnp.stack(
        [
            (wanted[:, None] == list_block[None, :]) & (rank[None, :] == 0),
            (wanted[:, None] == list_block[None, :]) & (rank[None, :] == 1),
            ref_index[:, None] == own_list[None, :],
        ],
        axis=1,
    ).reshape(3 * blocks, block_rows)
    outgoing = select_rows(chosen, records_owned[:, 0, :]).reshape(blocks, 3, samples)
    arrived = lax.all_to_all(outgoing, "chan", split_axis=0, concat_axis=0, tiled=True)
    inside = owner_lists // block_rows == own_block
    first = jnp.min(jnp.where(inside, owner_lists, blocks * block_rows), axis=1)
    second = jnp.max(jnp.where(inside, owner_lists, -1), axis=1)
    ids = jnp.stack([first, second, jnp.full_like(first, -1)], axis=1).reshape(3 * blocks)
    places = jnp.arange(block_rows)
    turned = own_block * block_rows + (places + segment * half_rows) % block_rows
    place = turned[:, None] == ids[None, :]
    panel_place = (jnp.arange(3 * blocks) % 3 == 2)[None, :]
    placed = select_rows(
        jnp.concatenate([place, panel_place], axis=0), arrived.reshape(3 * blocks, samples)
    )
    mine = placed[:half_rows]
    theirs = placed[half_rows:block_rows]
    swapped = lax.ppermute(theirs, "seg", [(0, 1), (1, 0)])
    pair = jnp.stack([mine, swapped])
    pair = jnp.where(segment == 0, pair, pair[::-1])
    panel_rows = lax.all_gather(placed[block_rows:], ("chan",), axis=0, tiled=True)
    series = lax.all_gather(pair, "lag", axis=1)
    panel = lax.all_gather(panel_rows, ("seg", "lag"), axis=0)
    parts = samples // LANES
    series = series.reshape(TILES // parts, half_rows, parts, LANES)
    series = series.transpose(0, 2, 1, 3).reshape(TILES, half_rows, LANES)
    panel = panel.reshape(TILES // parts, REF, parts, LANES)
    panel = panel.transpose(0, 2, 1, 3).reshape(TILES, REF, LANES)
    lag_width = LAGS // lax.axis_size("lag")
    groups = lag_width // COLUMN_LAGS
    return pl.pallas_call(
        correlate,
        out_shape=jax.ShapeDtypeStruct((half_rows, lag_width * REF), jnp.float32),
        in_specs=[pl.BlockSpec(memory_space=pltpu.VMEM)] * 2,
        out_specs=pl.BlockSpec(memory_space=pltpu.VMEM),
        scratch_shapes=[pltpu.VMEM((groups * half_rows, SAMPLES), jnp.bfloat16)] * 2
        + [pltpu.VMEM((COLUMN_LAGS * REF, SAMPLES), jnp.bfloat16)] * 2,
        compiler_params=pltpu.CompilerParams(vmem_limit_bytes=32 * 1024 * 1024),
        name="correlate",
    )(series, panel)


def solution(mesh):
    return jax.shard_map(
        shards,
        mesh=mesh,
        in_specs=(P("chan", "seg", "lag"), P(), P()),
        out_specs=P(("chan", "seg"), "lag"),
        check_vma=False,
    )
```

```python
import math

import jax
import jax.numpy as jnp
from jax import lax
from jax.experimental import pallas as pl
from jax.experimental.pallas import tpu as pltpu
from jax.sharding import PartitionSpec as P

MESH = pl.DeviceIdType.MESH
LAGS = 128
SAMPLES = 2048
REF = 64
TERMS = SAMPLES - LAGS
LANES = 128
TILES = SAMPLES // LANES
COLUMN_LAGS = 4
OWNERS = 64
ROWS = 128
HALF = 64
SEGMENTS = 2
LAG_PARTS = 4
Y, Z, CORES = 4, 8, 2
PARTS = 2
SENT = 6


def split(value):
    high = value.astype(jnp.bfloat16)
    return high, (value - high.astype(jnp.float32)).astype(jnp.bfloat16)


def transposed_dot(left, right):
    return lax.dot_general(
        left, right, (((1,), (1,)), ((), ())), preferred_element_type=jnp.float32
    )


def select_rows(chosen, values):
    one_hot = jnp.where(chosen, 1.0, 0.0).astype(jnp.bfloat16)
    high, low = split(values)
    return jnp.dot(one_hot, high, preferred_element_type=jnp.float32) + jnp.dot(
        one_hot, low, preferred_element_type=jnp.float32
    )


def iota(shape, dimension):
    return lax.broadcasted_iota(jnp.int32, shape, dimension)


def exchange(
    records_ref,
    lists_ref,
    refs_ref,
    series_ref,
    panel_ref,
    outgoing,
    arrived,
    rows_z,
    theirs,
    send_sems,
    recv_sems,
):
    me = lax.axis_index("chan")
    lag = lax.axis_index("lag")
    segment = lax.axis_index("seg")
    core = me % CORES
    z = (me // CORES) % Z
    y = me // (CORES * Z)
    along = segment * Z + z

    def owner(y_at, z_at, core_at):
        return (y_at * Z + z_at) * CORES + core_at

    def copy(source, target, number, **device):
        return pltpu.make_async_remote_copy(
            src_ref=source,
            dst_ref=target,
            send_sem=send_sems.at[number],
            recv_sem=recv_sems.at[number],
            device_id=device,
            device_id_type=MESH,
        )

    barrier = pltpu.get_barrier_semaphore()

    def greet_owner(step, carry):
        pl.semaphore_signal(
            barrier,
            inc=1,
            device_id={"chan": (me + step) % OWNERS},
            device_id_type=MESH,
        )
        return carry

    def greet_z(step, carry):
        pl.semaphore_signal(
            barrier,
            inc=1,
            device_id={"chan": owner(y, step, core), "seg": 1 - segment},
            device_id_type=MESH,
        )
        return carry

    lax.fori_loop(1, OWNERS, greet_owner, 0)
    lax.fori_loop(0, Z, greet_z, 0)
    for step in range(1, LAG_PARTS):
        pl.semaphore_signal(
            barrier,
            inc=1,
            device_id={"lag": (lag + step) % LAG_PARTS},
            device_id_type=MESH,
        )

    own = lists_ref[pl.ds(me, 1), :]
    own_down = jnp.transpose(jnp.broadcast_to(own.astype(jnp.float32), (ROWS, ROWS)))
    own_down = own_down.astype(jnp.int32)
    own_block = own // ROWS
    behind = (own_down // ROWS == own_block) & (own_down < own)
    rank = jnp.sum(jnp.where(behind, 1, 0), axis=0, keepdims=True)
    refs = refs_ref[...].astype(jnp.float32)
    refs_down = jnp.transpose(
        jnp.broadcast_to(jnp.concatenate([refs, refs], axis=1), (ROWS, ROWS))
    )[:REF].astype(jnp.int32)
    number = iota((REF, ROWS), 0)
    holder = owner((number // Z) % Y, number % Z, number // (Y * Z))
    panel_at = jnp.sum(
        jnp.where(refs_down == own, holder * 8 + 2 * PARTS + 1, 0), axis=0, keepdims=True
    ) - 1
    series_at = own_block * 8 + rank * PARTS
    series_at = jnp.concatenate([series_at, series_at + 1], axis=1)
    panel_at = jnp.concatenate([panel_at, jnp.where(panel_at < 0, -1, panel_at + 1)], axis=1)
    place = iota((OWNERS * 8, PARTS * ROWS), 0)
    records = jnp.concatenate(
        [records_ref[pl.ds(part, ROWS, PARTS), :] for part in range(PARTS)], axis=0
    )
    chosen = (place == series_at) | (place == panel_at)
    outgoing[...] = select_rows(chosen, records).reshape(OWNERS, 8, LANES)

    pl.semaphore_wait(barrier, OWNERS - 1 + Z + LAG_PARTS - 1)

    def send_owner(step, carry):
        peer = (me + step) % OWNERS
        copy(
            outgoing.at[peer, pl.ds(0, SENT)], arrived.at[me, pl.ds(0, SENT)], 0, chan=peer
        ).start()
        return carry

    lax.fori_loop(1, OWNERS, send_owner, 0)
    arrived[me] = outgoing[me]

    lists = lists_ref[...].astype(jnp.float32)
    lists = jnp.transpose(jnp.concatenate([lists, lists], axis=0)).astype(jnp.int32)
    inside = lists // ROWS == me
    first = jnp.min(jnp.where(inside, lists, OWNERS * ROWS), axis=0, keepdims=True)
    second = jnp.max(jnp.where(inside, lists, -1), axis=0, keepdims=True)
    ids = jnp.where(iota((1, ROWS), 1) < OWNERS, first, second)
    turned = me * ROWS + (iota((ROWS, ROWS), 0) + segment * HALF) % ROWS
    placing = turned == ids

    def wait_all(source, target, number):
        waiting = copy(source, target, number, lag=(lag + 1) % LAG_PARTS)
        waiting.wait_recv()

    def wait_sent(source, number):
        copy(source, source, number, lag=(lag + 1) % LAG_PARTS).wait_send()

    several = arrived.at[pl.ds(0, OWNERS - 1), pl.ds(0, SENT)]
    wait_all(several, several, 0)

    rows_z[along] = jnp.concatenate(
        [
            jnp.sum(arrived[:, 2 * PARTS + part, :], axis=0, keepdims=True)
            for part in range(PARTS)
        ],
        axis=0,
    )

    def send_z(step, carry):
        peer = (along + step) % (SEGMENTS * Z)
        copy(
            rows_z.at[along],
            rows_z.at[along],
            1,
            chan=owner(y, peer % Z, core),
            seg=peer // Z,
        ).start()
        return carry

    lax.fori_loop(1, SEGMENTS * Z, send_z, 0)

    placed = select_rows(
        placing,
        jnp.concatenate(
            [
                jnp.concatenate(
                    [arrived[:, slot * PARTS + part, :] for slot in range(2)], axis=0
                )
                for part in range(PARTS)
            ],
            axis=1,
        ),
    )
    own_tiles = pl.ds((segment * LAG_PARTS + lag) * PARTS, PARTS)
    other_tiles = pl.ds(((1 - segment) * LAG_PARTS + lag) * PARTS, PARTS)
    for part in range(PARTS):
        theirs[part] = placed[HALF:, part * LANES : (part + 1) * LANES]
    swap = copy(theirs, series_ref.at[own_tiles], 2, seg=1 - segment)
    swap.start()
    first_tile = (segment * LAG_PARTS + lag) * PARTS
    for part in range(PARTS):
        series_ref[first_tile + part] = placed[:HALF, part * LANES : (part + 1) * LANES]
    for step in range(1, LAG_PARTS):
        copy(
            series_ref.at[own_tiles],
            series_ref.at[own_tiles],
            3,
            lag=(lag + step) % LAG_PARTS,
        ).start()

    z_rows = rows_z.at[pl.ds(0, SEGMENTS * Z - 1)]
    wait_all(z_rows, z_rows, 1)
    group = core * Y + y
    lag_tiles = pl.ds(lag * PARTS, PARTS)
    group_rows = pl.ds(pl.multiple_of(group * Z, Z), Z)
    for at in range(SEGMENTS):
        for part in range(PARTS):
            panel_ref[at, lag * PARTS + part, group_rows, :] = rows_z[
                at * Z : (at + 1) * Z, part, :
            ]
    group_tiles = panel_ref.at[:, lag_tiles, group_rows]
    for step in range(1, Y):
        copy(group_tiles, group_tiles, 4, chan=owner((y + step) % Y, z, core)).start()
    y_tiles = panel_ref.at[:, pl.ds(0, PARTS), pl.ds(0, (Y - 1) * Z)]
    wait_all(y_tiles, y_tiles, 4)
    core_rows = pl.ds(pl.multiple_of(core * Y * Z, Y * Z), Y * Z)
    core_tiles = panel_ref.at[:, lag_tiles, core_rows]
    for step in range(1, LAG_PARTS):
        copy(core_tiles, core_tiles, 5, lag=(lag + step) % LAG_PARTS).start()

    swap.wait_recv()
    for step in range(1, LAG_PARTS):
        copy(
            series_ref.at[other_tiles],
            series_ref.at[other_tiles],
            6,
            lag=(lag + step) % LAG_PARTS,
        ).start()
    x_tiles = panel_ref.at[:, pl.ds(0, (LAG_PARTS - 1) * PARTS), pl.ds(0, Y * Z)]
    wait_all(x_tiles, x_tiles, 5)
    half_panel = panel_ref.at[:, :, core_rows]
    across = copy(half_panel, half_panel, 7, chan=owner(y, z, 1 - core))
    across.start()
    six = series_ref.at[pl.ds(0, (LAG_PARTS - 1) * PARTS)]
    wait_all(six, six, 3)
    wait_all(six, six, 6)
    across.wait()
    wait_sent(several, 0)
    wait_sent(z_rows, 1)
    swap.wait_send()
    wait_sent(six, 3)
    wait_sent(y_tiles, 4)
    wait_sent(x_tiles, 5)
    wait_sent(six, 6)


def correlate(series_ref, panel_ref, out_ref, windows_high, windows_low, shifts_high, shifts_low):
    lag_width = LAGS // LAG_PARTS
    rows = series_ref.shape[1]
    groups = lag_width // COLUMN_LAGS
    start = lax.axis_index("lag") * lag_width
    per_segment = TILES // SEGMENTS
    panel = jnp.concatenate(
        [panel_ref[tile // per_segment, tile % per_segment] for tile in range(TERMS // LANES)]
        + [jnp.zeros((REF, LANES), jnp.float32)] * (TILES - TERMS // LANES),
        axis=1,
    )
    panel = pltpu.roll(panel, start, 1)
    for shift in range(COLUMN_LAGS):
        high, low = split(pltpu.roll(panel, shift, 1) if shift else panel)
        shifts_high[pl.ds(shift * REF, REF), :] = high
        shifts_low[pl.ds(shift * REF, REF), :] = low
    series = jnp.concatenate([series_ref[tile] for tile in range(TILES)], axis=1)
    for group in range(groups):
        lag = group * COLUMN_LAGS
        high, low = split(pltpu.roll(series, SAMPLES - lag, 1) if lag else series)
        windows_high[pl.ds(group * rows, rows), :] = high
        windows_low[pl.ds(group * rows, rows), :] = low
    total = (
        transposed_dot(windows_high[...], shifts_high[...])
        + transposed_dot(windows_high[...], shifts_low[...])
        + transposed_dot(windows_low[...], shifts_high[...])
    )
    width = COLUMN_LAGS * REF
    for group in range(groups):
        out_ref[:, pl.ds(group * width, width)] = total[group * rows : (group + 1) * rows] * (
            1.0 / math.sqrt(TERMS)
        )


VMEM = pl.BlockSpec(memory_space=pltpu.VMEM)


def shards(records_owned, section_list, ref_index):
    series, panel = pl.pallas_call(
        exchange,
        out_shape=[
            jax.ShapeDtypeStruct((TILES, HALF, LANES), jnp.float32),
            jax.ShapeDtypeStruct((SEGMENTS, TILES // SEGMENTS, REF, LANES), jnp.float32),
        ],
        in_specs=[VMEM] * 3,
        out_specs=[VMEM] * 2,
        scratch_shapes=[
            pltpu.VMEM((OWNERS, 8, LANES), jnp.float32),
            pltpu.VMEM((OWNERS, 8, LANES), jnp.float32),
            pltpu.VMEM((SEGMENTS * Z, PARTS, LANES), jnp.float32),
            pltpu.VMEM((PARTS, HALF, LANES), jnp.float32),
            pltpu.SemaphoreType.DMA((8,)),
            pltpu.SemaphoreType.DMA((8,)),
        ],
        compiler_params=pltpu.CompilerParams(
            collective_id=0, has_side_effects=True, vmem_limit_bytes=32 * 1024 * 1024
        ),
        name="exchange",
    )(
        records_owned.reshape(ROWS * PARTS, LANES),
        section_list.reshape(OWNERS, ROWS),
        ref_index.reshape(1, REF),
    )
    lag_width = LAGS // LAG_PARTS
    groups = lag_width // COLUMN_LAGS
    return pl.pallas_call(
        correlate,
        out_shape=jax.ShapeDtypeStruct((HALF, lag_width * REF), jnp.float32),
        in_specs=[VMEM] * 2,
        out_specs=VMEM,
        scratch_shapes=[pltpu.VMEM((groups * HALF, SAMPLES), jnp.bfloat16)] * 2
        + [pltpu.VMEM((COLUMN_LAGS * REF, SAMPLES), jnp.bfloat16)] * 2,
        compiler_params=pltpu.CompilerParams(vmem_limit_bytes=32 * 1024 * 1024),
        name="correlate",
    )(series, panel)


def solution(mesh):
    return jax.shard_map(
        shards,
        mesh=mesh,
        in_specs=(P("chan", "seg", "lag"), P(), P()),
        out_specs=P(("chan", "seg"), "lag"),
        check_vma=False,
    )
```

```python
import math

import jax
import jax.numpy as jnp
from jax import lax
from jax.experimental import pallas as pl
from jax.experimental.pallas import tpu as pltpu
from jax.sharding import PartitionSpec as P

MESH = pl.DeviceIdType.MESH
LAGS = 128
SAMPLES = 2048
REF = 64
TERMS = SAMPLES - LAGS
LANES = 128
TILES = SAMPLES // LANES
COLUMN_LAGS = 4
OWNERS = 64
ROWS = 128
HALF = 64
SEGMENTS = 2
LAG_PARTS = 4
Y, Z, CORES = 4, 8, 2
PARTS = 2


def split(value):
    high = value.astype(jnp.bfloat16)
    return high, (value - high.astype(jnp.float32)).astype(jnp.bfloat16)


def transposed_dot(left, right):
    return lax.dot_general(
        left, right, (((1,), (1,)), ((), ())), preferred_element_type=jnp.float32
    )


def select_rows(chosen, values):
    one_hot = jnp.where(chosen, 1.0, 0.0).astype(jnp.bfloat16)
    high, low = split(values)
    return jnp.dot(one_hot, high, preferred_element_type=jnp.float32) + jnp.dot(
        one_hot, low, preferred_element_type=jnp.float32
    )


def iota(shape, dimension):
    return lax.broadcasted_iota(jnp.int32, shape, dimension)


def exchange(
    records_hbm,
    lists_hbm,
    refs_hbm,
    series_ref,
    panel_ref,
    records_ref,
    lists_ref,
    refs_ref,
    outgoing,
    arrived,
    rows_z,
    theirs,
    load_sems,
    send_sems,
    recv_sems,
):
    me = lax.axis_index("chan")
    lag = lax.axis_index("lag")
    segment = lax.axis_index("seg")
    core = me % CORES
    z = (me // CORES) % Z
    y = me // (CORES * Z)
    along = segment * Z + z

    def owner(y_at, z_at, core_at):
        return (y_at * Z + z_at) * CORES + core_at

    def copy(source, target, number, **device):
        return pltpu.make_async_remote_copy(
            src_ref=source,
            dst_ref=target,
            send_sem=send_sems.at[number],
            recv_sem=recv_sems.at[number],
            device_id=device,
            device_id_type=MESH,
        )

    def greet(**device):
        pl.semaphore_signal(barrier, inc=1, device_id=device, device_id_type=MESH)

    def wait_all(block, number):
        copy(block, block, number, lag=(lag + 1) % LAG_PARTS).wait_recv()

    def wait_sent(block, number):
        copy(block, block, number, lag=(lag + 1) % LAG_PARTS).wait_send()

    barrier = pltpu.get_barrier_semaphore()

    def greet_owner(step, carry):
        greet(chan=(me + step) % OWNERS)
        return carry

    def greet_z(step, carry):
        greet(chan=owner(y, step, core), seg=1 - segment)
        return carry

    loads = [
        pltpu.make_async_copy(source, target, load_sems.at[number])
        for number, (source, target) in enumerate(
            [(records_hbm, records_ref), (lists_hbm, lists_ref), (refs_hbm, refs_ref)]
        )
    ]
    for load in loads:
        load.start()
    lax.fori_loop(1, OWNERS, greet_owner, 0)
    lax.fori_loop(0, Z, greet_z, 0)
    for y_step in range(Y):
        for step in range(1, LAG_PARTS):
            greet(chan=owner((y + y_step) % Y, z, core), lag=(lag + step) % LAG_PARTS)
    for load in loads:
        load.wait()

    own = lists_ref[pl.ds(me, 1), :]
    own_down = jnp.transpose(jnp.broadcast_to(own.astype(jnp.float32), (ROWS, ROWS)))
    own_down = own_down.astype(jnp.int32)
    own_block = own // ROWS
    behind = (own_down // ROWS == own_block) & (own_down < own)
    rank = jnp.sum(jnp.where(behind, 1, 0), axis=0, keepdims=True)
    refs = refs_ref[...].astype(jnp.float32)
    refs_down = jnp.transpose(
        jnp.broadcast_to(jnp.concatenate([refs, refs], axis=1), (ROWS, ROWS))
    )[:REF].astype(jnp.int32)
    number = iota((REF, ROWS), 0)
    holder = owner((number // Z) % Y, number % Z, number // (Y * Z))
    panel_at = (
        jnp.sum(jnp.where(refs_down == own, holder * 8 + 1, 0), axis=0, keepdims=True) - 1
    )
    series_at = own_block * 8 + PARTS + rank
    series_at = jnp.concatenate([series_at, series_at + 2], axis=1)
    panel_at = jnp.concatenate([panel_at, jnp.where(panel_at < 0, -1, panel_at + 1)], axis=1)
    place = iota((OWNERS * 8, PARTS * ROWS), 0)
    records = jnp.concatenate(
        [records_ref[pl.ds(part, ROWS, PARTS), :] for part in range(PARTS)], axis=0
    )
    chosen = (place == series_at) | (place == panel_at)
    outgoing[...] = select_rows(chosen, records).reshape(OWNERS, 8, LANES)

    pl.semaphore_wait(barrier, OWNERS - 1 + Z + Y * (LAG_PARTS - 1))

    for stage in range(1 + PARTS):

        def send_owner(step, carry, pair=pl.ds(2 * stage, 2), stage=stage):
            peer = (me + step) % OWNERS
            copy(outgoing.at[peer, pair], arrived.at[me, pair], stage, chan=peer).start()
            return carry

        lax.fori_loop(1, OWNERS, send_owner, 0)
    arrived[me] = outgoing[me]

    lists = lists_ref[...].astype(jnp.float32)
    lists = jnp.transpose(jnp.concatenate([lists, lists], axis=0)).astype(jnp.int32)
    inside = lists // ROWS == me
    first = jnp.min(jnp.where(inside, lists, OWNERS * ROWS), axis=0, keepdims=True)
    second = jnp.max(jnp.where(inside, lists, -1), axis=0, keepdims=True)
    ids = jnp.where(iota((1, ROWS), 1) < OWNERS, first, second)
    turned = me * ROWS + (iota((ROWS, ROWS), 0) + segment * HALF) % ROWS
    placing = turned == ids
    pairs = [arrived.at[pl.ds(0, OWNERS - 1), pl.ds(2 * stage, 2)] for stage in range(1 + PARTS)]

    wait_all(pairs[0], 0)
    rows_z[along] = jnp.concatenate(
        [jnp.sum(arrived[:, part, :], axis=0, keepdims=True) for part in range(PARTS)], axis=0
    )

    def send_z(step, carry):
        peer = (along + step) % (SEGMENTS * Z)
        copy(
            rows_z.at[along],
            rows_z.at[along],
            3,
            chan=owner(y, peer % Z, core),
            seg=peer // Z,
        ).start()
        return carry

    lax.fori_loop(1, SEGMENTS * Z, send_z, 0)

    own_tile = (segment * LAG_PARTS + lag) * PARTS
    other_tile = ((1 - segment) * LAG_PARTS + lag) * PARTS
    swaps = [
        copy(theirs.at[part], series_ref.at[own_tile + part], 6 + part, seg=1 - segment)
        for part in range(PARTS)
    ]

    def forward(tile, number):
        for step in range(1, LAG_PARTS):
            copy(
                series_ref.at[tile], series_ref.at[tile], number, lag=(lag + step) % LAG_PARTS
            ).start()

    def place_part(part):
        wait_all(pairs[1 + part], 1 + part)
        placed = select_rows(
            placing,
            jnp.concatenate(
                [arrived[:, PARTS * (1 + part) + slot, :] for slot in range(2)], axis=0
            ),
        )
        theirs[part] = placed[HALF:]
        swaps[part].start()
        series_ref[own_tile + part] = placed[:HALF]
        forward(own_tile + part, 8 + part)

    place_part(0)

    z_rows = rows_z.at[pl.ds(0, SEGMENTS * Z - 1)]
    wait_all(z_rows, 3)
    lag_tiles = pl.ds(lag * PARTS, PARTS)
    group_rows = pl.ds(pl.multiple_of((core * Y + y) * Z, Z), Z)
    for at in range(SEGMENTS):
        for part in range(PARTS):
            panel_ref[at, lag * PARTS + part, group_rows, :] = rows_z[
                at * Z : (at + 1) * Z, part, :
            ]
    group_tiles = panel_ref.at[:, lag_tiles, group_rows]
    for y_step in range(Y):
        for step in range(LAG_PARTS):
            if y_step or step:
                copy(
                    group_tiles,
                    group_tiles,
                    4,
                    chan=owner((y + y_step) % Y, z, core),
                    lag=(lag + step) % LAG_PARTS,
                ).start()

    place_part(1)
    for part in range(PARTS):
        swaps[part].wait_recv()
        forward(other_tile + part, 10 + part)

    xy_tiles = panel_ref.at[:, pl.ds(0, 5), pl.ds(0, 6 * Z)]
    wait_all(xy_tiles, 4)
    core_rows = pl.ds(pl.multiple_of(core * Y * Z, Y * Z), Y * Z)
    half_panel = panel_ref.at[:, :, core_rows]
    across = copy(half_panel, half_panel, 5, chan=owner(y, z, 1 - core))
    across.start()
    three = series_ref.at[pl.ds(0, LAG_PARTS - 1)]
    for number in range(8, 12):
        wait_all(three, number)
    across.wait()
    for stage in range(1 + PARTS):
        wait_sent(pairs[stage], stage)
    wait_sent(z_rows, 3)
    wait_sent(xy_tiles, 4)
    for part in range(PARTS):
        swaps[part].wait_send()
    for number in range(8, 12):
        wait_sent(three, number)


def correlate(series_ref, panel_ref, out_ref, windows_high, windows_low, shifts_high, shifts_low):
    lag_width = LAGS // LAG_PARTS
    rows = series_ref.shape[1]
    groups = lag_width // COLUMN_LAGS
    start = lax.axis_index("lag") * lag_width
    per_segment = TILES // SEGMENTS
    panel = jnp.concatenate(
        [panel_ref[tile // per_segment, tile % per_segment] for tile in range(TERMS // LANES)]
        + [jnp.zeros((REF, LANES), jnp.float32)] * (TILES - TERMS // LANES),
        axis=1,
    )
    panel = pltpu.roll(panel, start, 1)
    for shift in range(COLUMN_LAGS):
        high, low = split(pltpu.roll(panel, shift, 1) if shift else panel)
        shifts_high[pl.ds(shift * REF, REF), :] = high
        shifts_low[pl.ds(shift * REF, REF), :] = low
    series = jnp.concatenate([series_ref[tile] for tile in range(TILES)], axis=1)
    for group in range(groups):
        lag = group * COLUMN_LAGS
        high, low = split(pltpu.roll(series, SAMPLES - lag, 1) if lag else series)
        windows_high[pl.ds(group * rows, rows), :] = high
        windows_low[pl.ds(group * rows, rows), :] = low
    total = (
        transposed_dot(windows_high[...], shifts_high[...])
        + transposed_dot(windows_high[...], shifts_low[...])
        + transposed_dot(windows_low[...], shifts_high[...])
    )
    width = COLUMN_LAGS * REF
    for group in range(groups):
        out_ref[:, pl.ds(group * width, width)] = total[group * rows : (group + 1) * rows] * (
            1.0 / math.sqrt(TERMS)
        )


VMEM = pl.BlockSpec(memory_space=pltpu.VMEM)


def shards(records_owned, section_list, ref_index):
    series, panel = pl.pallas_call(
        exchange,
        out_shape=[
            jax.ShapeDtypeStruct((TILES, HALF, LANES), jnp.float32),
            jax.ShapeDtypeStruct((SEGMENTS, TILES // SEGMENTS, REF, LANES), jnp.float32),
        ],
        in_specs=[pl.BlockSpec(memory_space=pltpu.HBM)] * 3,
        out_specs=[VMEM] * 2,
        scratch_shapes=[
            pltpu.VMEM((ROWS * PARTS, LANES), jnp.float32),
            pltpu.VMEM((OWNERS, ROWS), jnp.int32),
            pltpu.VMEM((1, REF), jnp.int32),
            pltpu.VMEM((OWNERS, 8, LANES), jnp.float32),
            pltpu.VMEM((OWNERS, 8, LANES), jnp.float32),
            pltpu.VMEM((SEGMENTS * Z, PARTS, LANES), jnp.float32),
            pltpu.VMEM((PARTS, HALF, LANES), jnp.float32),
            pltpu.SemaphoreType.DMA((3,)),
            pltpu.SemaphoreType.DMA((12,)),
            pltpu.SemaphoreType.DMA((12,)),
        ],
        compiler_params=pltpu.CompilerParams(
            collective_id=0, has_side_effects=True, vmem_limit_bytes=32 * 1024 * 1024
        ),
        name="exchange",
    )(
        *[
            pltpu.with_memory_space_constraint(value, pltpu.HBM)
            for value in (
                records_owned.reshape(ROWS * PARTS, LANES),
                section_list.reshape(OWNERS, ROWS),
                ref_index.reshape(1, REF),
            )
        ]
    )
    lag_width = LAGS // LAG_PARTS
    groups = lag_width // COLUMN_LAGS
    return pl.pallas_call(
        correlate,
        out_shape=jax.ShapeDtypeStruct((HALF, lag_width * REF), jnp.float32),
        in_specs=[VMEM] * 2,
        out_specs=VMEM,
        scratch_shapes=[pltpu.VMEM((groups * HALF, SAMPLES), jnp.bfloat16)] * 2
        + [pltpu.VMEM((COLUMN_LAGS * REF, SAMPLES), jnp.bfloat16)] * 2,
        compiler_params=pltpu.CompilerParams(vmem_limit_bytes=32 * 1024 * 1024),
        name="correlate",
    )(series, panel)


def solution(mesh):
    return jax.shard_map(
        shards,
        mesh=mesh,
        in_specs=(P("chan", "seg", "lag"), P(), P()),
        out_specs=P(("chan", "seg"), "lag"),
        check_vma=False,
    )
```

```python
import math

import jax
import jax.numpy as jnp
from jax import lax
from jax.experimental import pallas as pl
from jax.experimental.pallas import tpu as pltpu
from jax.sharding import PartitionSpec as P

MESH = pl.DeviceIdType.MESH
LAGS = 128
SAMPLES = 2048
REF = 64
TERMS = SAMPLES - LAGS
LANES = 128
TILES = SAMPLES // LANES
COLUMN_LAGS = 4
OWNERS = 64
ROWS = 128
HALF = 64
SEGMENTS = 2
LAG_PARTS = 4
Y, Z, CORES = 4, 8, 2
WIDE = Y * CORES
PARTS = 2


def split(value):
    high = value.astype(jnp.bfloat16)
    return high, (value - high.astype(jnp.float32)).astype(jnp.bfloat16)


def transposed_dot(left, right):
    return lax.dot_general(
        left, right, (((1,), (1,)), ((), ())), preferred_element_type=jnp.float32
    )


def select_rows(chosen, values):
    one_hot = jnp.where(chosen, 1.0, 0.0).astype(jnp.bfloat16)
    high, low = split(values)
    return jnp.dot(one_hot, high, preferred_element_type=jnp.float32) + jnp.dot(
        one_hot, low, preferred_element_type=jnp.float32
    )


def iota(shape, dimension):
    return lax.broadcasted_iota(jnp.int32, shape, dimension)


def exchange(
    records_hbm,
    lists_hbm,
    refs_hbm,
    series_ref,
    panel_ref,
    records_ref,
    lists_ref,
    refs_ref,
    outgoing,
    across_plane,
    line_out,
    along_line,
    sums_out,
    sums_in,
    rows_z,
    theirs,
    load_sems,
    send_sems,
    recv_sems,
):
    me = lax.axis_index("chan")
    lag = lax.axis_index("lag")
    segment = lax.axis_index("seg")
    core = me % CORES
    z = (me // CORES) % Z
    y = me // (CORES * Z)
    along = segment * Z + z

    def owner(y_at, z_at, core_at):
        return (y_at * Z + z_at) * CORES + core_at

    wide = y * CORES + core

    def plane_peer(step):
        at = (wide + step) % WIDE
        return owner(at // CORES, z, at % CORES)

    def line_peer(step):
        at = (along + step) % (SEGMENTS * Z)
        return {"chan": owner(y, at % Z, core), "seg": at // Z}

    def copy(source, target, number, **device):
        return pltpu.make_async_remote_copy(
            src_ref=source,
            dst_ref=target,
            send_sem=send_sems.at[number],
            recv_sem=recv_sems.at[number],
            device_id=device,
            device_id_type=MESH,
        )

    def greet(**device):
        pl.semaphore_signal(barrier, inc=1, device_id=device, device_id_type=MESH)

    def wait_all(block, number):
        copy(block, block, number, lag=(lag + 1) % LAG_PARTS).wait_recv()

    def wait_sent(block, number):
        copy(block, block, number, lag=(lag + 1) % LAG_PARTS).wait_send()

    barrier = pltpu.get_barrier_semaphore()

    loads = [
        pltpu.make_async_copy(source, target, load_sems.at[number])
        for number, (source, target) in enumerate(
            [(records_hbm, records_ref), (lists_hbm, lists_ref), (refs_hbm, refs_ref)]
        )
    ]
    for load in loads:
        load.start()
    for step in range(1, WIDE):
        greet(chan=plane_peer(step))
    for step in range(1, SEGMENTS * Z):
        greet(**line_peer(step))
    for y_step in range(Y):
        for step in range(1, LAG_PARTS):
            greet(chan=owner((y + y_step) % Y, z, core), lag=(lag + step) % LAG_PARTS)
    for load in loads:
        load.wait()

    own = lists_ref[pl.ds(me, 1), :]
    own_down = jnp.transpose(jnp.broadcast_to(own.astype(jnp.float32), (ROWS, ROWS)))
    own_down = own_down.astype(jnp.int32)
    own_block = own // ROWS
    behind = (own_down // ROWS == own_block) & (own_down < own)
    rank = jnp.sum(jnp.where(behind, 1, 0), axis=0, keepdims=True)
    refs = refs_ref[...].astype(jnp.float32)
    refs_down = jnp.transpose(
        jnp.broadcast_to(jnp.concatenate([refs, refs], axis=1), (ROWS, ROWS))
    )[:REF].astype(jnp.int32)
    number = iota((REF, ROWS), 0)
    number = number // (Y * Z) + (number // Z) % Y * CORES, number % Z
    panel_at = (
        jnp.sum(
            jnp.where(refs_down == own, (number[0] * Z + number[1]) * 2 + 1, 0),
            axis=0,
            keepdims=True,
        )
        - 1
    )
    own_wide = own_block // (Z * CORES) * CORES + own_block % CORES
    series_at = (own_wide * Z + own_block // CORES % Z) * 2 + rank
    series_at = jnp.concatenate([series_at + ROWS, series_at + 2 * ROWS], axis=1)
    panel_at = jnp.concatenate([panel_at, jnp.where(panel_at < 0, -1, panel_at + 1)], axis=1)
    place = iota(((1 + PARTS) * ROWS, PARTS * ROWS), 0)
    records = jnp.concatenate(
        [records_ref[pl.ds(part, ROWS, PARTS), :] for part in range(PARTS)], axis=0
    )
    chosen = (place == series_at) | (place == panel_at)
    outgoing[...] = select_rows(chosen, records).reshape(1 + PARTS, WIDE, 2 * Z, LANES)

    pl.semaphore_wait(barrier, WIDE - 1 + SEGMENTS * Z - 1 + Y * (LAG_PARTS - 1))

    for kind in range(1 + PARTS):
        for step in range(1, WIDE):
            at = (wide + step) % WIDE
            copy(
                outgoing.at[kind, at], across_plane.at[kind, wide], kind, chan=plane_peer(step)
            ).start()
        across_plane[kind, wide] = outgoing[kind, wide]

    lists = lists_ref[...].astype(jnp.float32)
    lists = jnp.transpose(jnp.concatenate([lists, lists], axis=0)).astype(jnp.int32)
    inside = lists // ROWS == me
    first = jnp.min(jnp.where(inside, lists, OWNERS * ROWS), axis=0, keepdims=True)
    second = jnp.max(jnp.where(inside, lists, -1), axis=0, keepdims=True)
    ids = jnp.where(iota((1, ROWS), 1) < OWNERS, first, second)
    turned = me * ROWS + (iota((ROWS, ROWS), 0) + segment * HALF) % ROWS
    down, right = iota((ROWS, ROWS), 0), iota((ROWS, ROWS), 1)
    right_wide = right // 2 % WIDE
    right_owner = owner(right_wide // CORES, right // (2 * WIDE), right_wide % CORES)
    reorder = jnp.where(down == right % 2 * OWNERS + right_owner, 1.0, 0.0).astype(jnp.bfloat16)
    placing = (
        jnp.dot(
            jnp.where(turned == ids, 1.0, 0.0).astype(jnp.bfloat16),
            reorder,
            preferred_element_type=jnp.float32,
        )
        > 0.5
    )
    by_line = right == (down // 2 % WIDE * Z + down // (2 * WIDE)) * 2 + down % 2

    seven_plane = [across_plane.at[kind, pl.ds(0, WIDE - 1)] for kind in range(1 + PARTS)]
    seven_line = along_line.at[0, pl.ds(0, Z - 1)]

    wait_all(seven_plane[0], 0)
    sums = jnp.sum(across_plane[0], axis=0)
    for at in range(Z):
        sums_out[at] = sums[2 * at : 2 * at + 2]
    for step in range(1, Z):
        at = (z + step) % Z
        copy(sums_out.at[at], sums_in.at[z], 3, chan=owner(y, at, core)).start()
    sums_in[z] = sums_out[z]

    def send_line(part):
        wait_all(seven_plane[1 + part], 1 + part)
        line_out[part] = select_rows(
            by_line, across_plane[1 + part].reshape(ROWS, LANES)
        ).reshape(Z, 2 * WIDE, LANES)
        for step in range(1, Z):
            at = (z + step) % Z
            copy(
                line_out.at[part, at], along_line.at[part, z], 4 + part, chan=owner(y, at, core)
            ).start()
        along_line[part, z] = line_out[part, z]

    send_line(0)
    send_line(1)

    seven_sums = sums_in.at[pl.ds(0, Z - 1)]
    wait_all(seven_sums, 3)
    rows_z[along] = jnp.sum(sums_in[...], axis=0)
    for step in range(1, SEGMENTS * Z):
        copy(rows_z.at[along], rows_z.at[along], 6, **line_peer(step)).start()

    own_tile = (segment * LAG_PARTS + lag) * PARTS
    other_tile = ((1 - segment) * LAG_PARTS + lag) * PARTS
    swaps = [
        copy(theirs.at[part], series_ref.at[own_tile + part], 9 + part, seg=1 - segment)
        for part in range(PARTS)
    ]

    def forward(tile, number):
        for step in range(1, LAG_PARTS):
            copy(
                series_ref.at[tile], series_ref.at[tile], number, lag=(lag + step) % LAG_PARTS
            ).start()

    def place_part(part):
        wait_all(seven_line, 4 + part)
        placed = select_rows(placing, along_line[part].reshape(ROWS, LANES))
        theirs[part] = placed[HALF:]

        @pl.when(segment == 1)
        def _():
            swaps[part].start()

        series_ref[own_tile + part] = placed[:HALF]
        forward(own_tile + part, 11 + part)

    place_part(0)

    z_rows = rows_z.at[pl.ds(0, SEGMENTS * Z - 1)]
    wait_all(z_rows, 6)
    lag_tiles = pl.ds(lag * PARTS, PARTS)
    group_rows = pl.ds(pl.multiple_of((core * Y + y) * Z, Z), Z)
    for at in range(SEGMENTS):
        for part in range(PARTS):
            panel_ref[at, lag * PARTS + part, group_rows, :] = rows_z[
                at * Z : (at + 1) * Z, part, :
            ]
    group_tiles = panel_ref.at[:, lag_tiles, group_rows]
    for y_step in range(Y):
        for step in range(LAG_PARTS):
            if y_step or step:
                copy(
                    group_tiles,
                    group_tiles,
                    7,
                    chan=owner((y + y_step) % Y, z, core),
                    lag=(lag + step) % LAG_PARTS,
                ).start()

    place_part(1)
    for part in range(PARTS):
        swaps[part].wait_recv()
        forward(other_tile + part, 13 + part)

    @pl.when(segment == 0)
    def _():
        for part in range(PARTS):
            swaps[part].start()

    xy_tiles = panel_ref.at[:, pl.ds(0, 5), pl.ds(0, 6 * Z)]
    wait_all(xy_tiles, 7)
    core_rows = pl.ds(pl.multiple_of(core * Y * Z, Y * Z), Y * Z)
    half_panel = panel_ref.at[:, :, core_rows]
    across = copy(half_panel, half_panel, 8, chan=owner(y, z, 1 - core))
    across.start()
    three = series_ref.at[pl.ds(0, LAG_PARTS - 1)]
    for number in range(11, 15):
        wait_all(three, number)
    across.wait()
    for kind in range(1 + PARTS):
        wait_sent(seven_plane[kind], kind)
    wait_sent(seven_sums, 3)
    for part in range(PARTS):
        wait_sent(seven_line, 4 + part)
        swaps[part].wait_send()
    wait_sent(z_rows, 6)
    wait_sent(xy_tiles, 7)
    for number in range(11, 15):
        wait_sent(three, number)


def correlate(series_ref, panel_ref, out_ref, windows_high, windows_low, shifts_high, shifts_low):
    lag_width = LAGS // LAG_PARTS
    rows = series_ref.shape[1]
    groups = lag_width // COLUMN_LAGS
    start = lax.axis_index("lag") * lag_width
    per_segment = TILES // SEGMENTS
    panel = jnp.concatenate(
        [panel_ref[tile // per_segment, tile % per_segment] for tile in range(TERMS // LANES)]
        + [jnp.zeros((REF, LANES), jnp.float32)] * (TILES - TERMS // LANES),
        axis=1,
    )
    panel = pltpu.roll(panel, start, 1)
    for shift in range(COLUMN_LAGS):
        high, low = split(pltpu.roll(panel, shift, 1) if shift else panel)
        shifts_high[pl.ds(shift * REF, REF), :] = high
        shifts_low[pl.ds(shift * REF, REF), :] = low
    series = jnp.concatenate([series_ref[tile] for tile in range(TILES)], axis=1)
    for group in range(groups):
        lag = group * COLUMN_LAGS
        high, low = split(pltpu.roll(series, SAMPLES - lag, 1) if lag else series)
        windows_high[pl.ds(group * rows, rows), :] = high
        windows_low[pl.ds(group * rows, rows), :] = low
    total = (
        transposed_dot(windows_high[...], shifts_high[...])
        + transposed_dot(windows_high[...], shifts_low[...])
        + transposed_dot(windows_low[...], shifts_high[...])
    )
    width = COLUMN_LAGS * REF
    for group in range(groups):
        out_ref[:, pl.ds(group * width, width)] = total[group * rows : (group + 1) * rows] * (
            1.0 / math.sqrt(TERMS)
        )


VMEM = pl.BlockSpec(memory_space=pltpu.VMEM)


def shards(records_owned, section_list, ref_index):
    series, panel = pl.pallas_call(
        exchange,
        out_shape=[
            jax.ShapeDtypeStruct((TILES, HALF, LANES), jnp.float32),
            jax.ShapeDtypeStruct((SEGMENTS, TILES // SEGMENTS, REF, LANES), jnp.float32),
        ],
        in_specs=[pl.BlockSpec(memory_space=pltpu.HBM)] * 3,
        out_specs=[VMEM] * 2,
        scratch_shapes=[
            pltpu.VMEM((ROWS * PARTS, LANES), jnp.float32),
            pltpu.VMEM((OWNERS, ROWS), jnp.int32),
            pltpu.VMEM((1, REF), jnp.int32),
            pltpu.VMEM((1 + PARTS, WIDE, 2 * Z, LANES), jnp.float32),
            pltpu.VMEM((1 + PARTS, WIDE, 2 * Z, LANES), jnp.float32),
            pltpu.VMEM((PARTS, Z, 2 * WIDE, LANES), jnp.float32),
            pltpu.VMEM((PARTS, Z, 2 * WIDE, LANES), jnp.float32),
            pltpu.VMEM((Z, PARTS, LANES), jnp.float32),
            pltpu.VMEM((Z, PARTS, LANES), jnp.float32),
            pltpu.VMEM((SEGMENTS * Z, PARTS, LANES), jnp.float32),
            pltpu.VMEM((PARTS, HALF, LANES), jnp.float32),
            pltpu.SemaphoreType.DMA((3,)),
            pltpu.SemaphoreType.DMA((15,)),
            pltpu.SemaphoreType.DMA((15,)),
        ],
        compiler_params=pltpu.CompilerParams(
            collective_id=0, has_side_effects=True, vmem_limit_bytes=32 * 1024 * 1024
        ),
        name="exchange",
    )(
        *[
            pltpu.with_memory_space_constraint(value, pltpu.HBM)
            for value in (
                records_owned.reshape(ROWS * PARTS, LANES),
                section_list.reshape(OWNERS, ROWS),
                ref_index.reshape(1, REF),
            )
        ]
    )
    lag_width = LAGS // LAG_PARTS
    groups = lag_width // COLUMN_LAGS
    return pl.pallas_call(
        correlate,
        out_shape=jax.ShapeDtypeStruct((HALF, lag_width * REF), jnp.float32),
        in_specs=[VMEM] * 2,
        out_specs=VMEM,
        scratch_shapes=[pltpu.VMEM((groups * HALF, SAMPLES), jnp.bfloat16)] * 2
        + [pltpu.VMEM((COLUMN_LAGS * REF, SAMPLES), jnp.bfloat16)] * 2,
        compiler_params=pltpu.CompilerParams(vmem_limit_bytes=32 * 1024 * 1024),
        name="correlate",
    )(series, panel)


def solution(mesh):
    return jax.shard_map(
        shards,
        mesh=mesh,
        in_specs=(P("chan", "seg", "lag"), P(), P()),
        out_specs=P(("chan", "seg"), "lag"),
        check_vma=False,
    )
```

```python
import math

import jax
import jax.numpy as jnp
from jax import lax
from jax.experimental import pallas as pl
from jax.experimental.pallas import tpu as pltpu
from jax.sharding import PartitionSpec as P

MESH = pl.DeviceIdType.MESH
LAGS = 128
SAMPLES = 2048
REF = 64
TERMS = SAMPLES - LAGS
LANES = 128
TILES = SAMPLES // LANES
COLUMN_LAGS = 4
OWNERS = 64
ROWS = 128
HALF = 64
SEGMENTS = 2
LAG_PARTS = 4
Y, Z, CORES = 4, 8, 2
WIDE = Y * CORES
NEAR = 2
KEPT = Z // NEAR
PARTS = 2


def split(value):
    high = value.astype(jnp.bfloat16)
    return high, (value - high.astype(jnp.float32)).astype(jnp.bfloat16)


def transposed_dot(left, right):
    return lax.dot_general(
        left, right, (((1,), (1,)), ((), ())), preferred_element_type=jnp.float32
    )


def select_rows(chosen, values):
    one_hot = jnp.where(chosen, 1.0, 0.0).astype(jnp.bfloat16)
    high, low = split(values)
    return jnp.dot(one_hot, high, preferred_element_type=jnp.float32) + jnp.dot(
        one_hot, low, preferred_element_type=jnp.float32
    )


def iota(shape, dimension):
    return lax.broadcasted_iota(jnp.int32, shape, dimension)


def exchange(
    records_hbm,
    lists_hbm,
    refs_hbm,
    series_ref,
    panel_ref,
    records_ref,
    lists_ref,
    refs_ref,
    panel_out,
    panel_in,
    outgoing,
    across_plane,
    line_out,
    along_line,
    sums,
    theirs,
    late_sem,
    load_sems,
    send_sems,
    recv_sems,
):
    me = lax.axis_index("chan")
    lag = lax.axis_index("lag")
    segment = lax.axis_index("seg")
    core = me % CORES
    z = (me // CORES) % Z
    y = me // (CORES * Z)
    along = segment * Z + z

    def owner(y_at, z_at, core_at):
        return (y_at * Z + z_at) * CORES + core_at

    wide = y * CORES + core

    def plane_peer(step):
        at = (wide + step) % WIDE
        return owner(at // CORES, z, at % CORES)

    first_near = z // NEAR * NEAR
    near = wide * NEAR + z % NEAR

    def near_peer(step):
        at = (near + step) % (WIDE * NEAR)
        at_wide = at // NEAR
        return at, owner(at_wide // CORES, first_near + at % NEAR, at_wide % CORES)

    def copy(source, target, number, **device):
        return pltpu.make_async_remote_copy(
            src_ref=source,
            dst_ref=target,
            send_sem=send_sems.at[number],
            recv_sem=recv_sems.at[number],
            device_id=device,
            device_id_type=MESH,
        )

    def greet(**device):
        pl.semaphore_signal(barrier, inc=1, device_id=device, device_id_type=MESH)

    def wait_all(block, number):
        copy(block, block, number, lag=(lag + 1) % LAG_PARTS).wait_recv()

    def wait_sent(block, number):
        copy(block, block, number, lag=(lag + 1) % LAG_PARTS).wait_send()

    barrier = pltpu.get_barrier_semaphore()

    loads = [
        pltpu.make_async_copy(source, target, load_sems.at[number])
        for number, (source, target) in enumerate(
            [(records_hbm, records_ref), (lists_hbm, lists_ref), (refs_hbm, refs_ref)]
        )
    ]
    for load in loads:
        load.start()

    @pl.when(segment == 0)
    def _():
        for step in range(Z):
            greet(chan=owner(y, step, core), seg=1)

    for step in range(1, WIDE * NEAR):
        greet(chan=near_peer(step)[1])
    for step in range(1, Z // NEAR):
        for at in range(NEAR):
            greet(chan=owner(y, (first_near + step * NEAR + at) % Z, core))
    for y_step in range(Y):
        for step in range(1, LAG_PARTS):
            greet(chan=owner((y + y_step) % Y, z, core), lag=(lag + step) % LAG_PARTS)
    for load in loads:
        load.wait()

    own = lists_ref[pl.ds(me, 1), :]
    own_down = jnp.transpose(jnp.broadcast_to(own.astype(jnp.float32), (ROWS, ROWS)))
    own_down = own_down.astype(jnp.int32)
    own_block = own // ROWS
    behind = (own_down // ROWS == own_block) & (own_down < own)
    rank = jnp.sum(jnp.where(behind, 1, 0), axis=0, keepdims=True)
    refs = refs_ref[...].astype(jnp.float32)
    refs_down = jnp.transpose(
        jnp.broadcast_to(jnp.concatenate([refs, refs], axis=1), (ROWS, ROWS))
    )[:REF].astype(jnp.int32)
    number = iota((REF, ROWS), 0)
    target = (number // (Y * Z) + (number // Z) % Y * CORES) * NEAR + number % Z // KEPT
    panel_at = jnp.sum(
        jnp.where(refs_down == own, target * 8 + number % KEPT + 1, 0), axis=0, keepdims=True
    )
    panel_at = panel_at - 1
    own_wide = own_block // (Z * CORES) * CORES + own_block % CORES
    series_at = (own_wide * Z + own_block // CORES % Z) * 2 + rank
    series_at = jnp.concatenate([series_at, series_at + ROWS], axis=1)
    panel_at = jnp.concatenate([panel_at, jnp.where(panel_at < 0, -1, panel_at + KEPT)], axis=1)
    place = iota((PARTS * ROWS, PARTS * ROWS), 0)
    panel_place = iota((WIDE * NEAR * 8, PARTS * ROWS), 0)
    records = jnp.concatenate(
        [records_ref[pl.ds(part, ROWS, PARTS), :] for part in range(PARTS)], axis=0
    )
    panel_out[...] = select_rows(panel_place == panel_at, records).reshape(WIDE * NEAR, 8, LANES)
    outgoing[...] = select_rows(place == series_at, records).reshape(PARTS, WIDE, 2 * Z, LANES)

    pl.semaphore_wait(barrier, WIDE * NEAR - 1 + Z - NEAR + Y * (LAG_PARTS - 1) + Z * segment)

    kept = pl.ds(0, PARTS * KEPT)
    for step in range(1, WIDE * NEAR):
        at, peer = near_peer(step)
        copy(panel_out.at[at, kept], panel_in.at[near, kept], 0, chan=peer).start()
    panel_in[near] = panel_out[near]

    @pl.when(segment == 1)
    def _():
        for step in range(Z):
            pl.semaphore_signal(
                late_sem,
                inc=1,
                device_id={"chan": owner(y, step, core), "seg": 0},
                device_id_type=MESH,
            )

    for part in range(PARTS):
        for step in range(1, WIDE):
            at = (wide + step) % WIDE
            copy(
                outgoing.at[part, at],
                across_plane.at[part, wide],
                1 + part,
                chan=plane_peer(step),
            ).start()
        across_plane[part, wide] = outgoing[part, wide]

    lists = lists_ref[...].astype(jnp.float32)
    lists = jnp.transpose(jnp.concatenate([lists, lists], axis=0)).astype(jnp.int32)
    inside = lists // ROWS == me
    first = jnp.min(jnp.where(inside, lists, OWNERS * ROWS), axis=0, keepdims=True)
    second = jnp.max(jnp.where(inside, lists, -1), axis=0, keepdims=True)
    ids = jnp.where(iota((1, ROWS), 1) < OWNERS, first, second)
    turned = me * ROWS + (iota((ROWS, ROWS), 0) + segment * HALF) % ROWS
    down, right = iota((ROWS, ROWS), 0), iota((ROWS, ROWS), 1)
    right_wide = right // 2 % WIDE
    right_owner = owner(right_wide // CORES, right // (2 * WIDE), right_wide % CORES)
    reorder = jnp.where(down == right % 2 * OWNERS + right_owner, 1.0, 0.0).astype(jnp.bfloat16)
    placing = (
        jnp.dot(
            jnp.where(turned == ids, 1.0, 0.0).astype(jnp.bfloat16),
            reorder,
            preferred_element_type=jnp.float32,
        )
        > 0.5
    )
    by_line = right == (down // 2 % WIDE * Z + down // (2 * WIDE)) * 2 + down % 2

    seven_plane = [across_plane.at[part, pl.ds(0, WIDE - 1)] for part in range(PARTS)]
    near_others = panel_in.at[pl.ds(0, WIDE * NEAR - 1), kept]
    seven_line = along_line.at[0, pl.ds(0, Z - 1)]

    wait_all(near_others, 0)
    sums[along, kept] = jnp.sum(panel_in[:, kept], axis=0)
    for step in range(1, Z):
        copy(
            sums.at[along, kept], sums.at[along, kept], 3, chan=owner(y, (z + step) % Z, core)
        ).start()

    def send_sums_over():
        for step in range(Z):
            copy(
                sums.at[along, kept],
                sums.at[along, kept],
                15,
                chan=owner(y, (z + step) % Z, core),
                seg=1 - segment,
            ).start()

    @pl.when(segment == 1)
    def _():
        send_sums_over()

    def send_line(part):
        wait_all(seven_plane[part], 1 + part)
        line_out[part] = select_rows(
            by_line, across_plane[part].reshape(ROWS, LANES)
        ).reshape(Z, 2 * WIDE, LANES)
        for step in range(1, Z):
            at = (z + step) % Z
            copy(
                line_out.at[part, at], along_line.at[part, z], 4 + part, chan=owner(y, at, core)
            ).start()
        along_line[part, z] = line_out[part, z]

    send_line(0)
    send_line(1)

    own_tile = (segment * LAG_PARTS + lag) * PARTS
    other_tile = ((1 - segment) * LAG_PARTS + lag) * PARTS
    swaps = [
        copy(theirs.at[part], series_ref.at[own_tile + part], 9 + part, seg=1 - segment)
        for part in range(PARTS)
    ]

    def forward(tile, number):
        for step in range(1, LAG_PARTS):
            copy(
                series_ref.at[tile], series_ref.at[tile], number, lag=(lag + step) % LAG_PARTS
            ).start()

    def place_part(part):
        wait_all(seven_line, 4 + part)
        placed = select_rows(placing, along_line[part].reshape(ROWS, LANES))
        theirs[part] = placed[HALF:]
        if part == 0:

            @pl.when(segment == 0)
            def _():
                pl.semaphore_wait(late_sem, Z)

        swaps[part].start()
        series_ref[own_tile + part] = placed[:HALF]
        forward(own_tile + part, 11 + part)

    place_part(0)
    place_part(1)

    @pl.when(segment == 0)
    def _():
        send_sums_over()

    lag_tiles = pl.ds(lag * PARTS, PARTS)
    group_rows = pl.ds(pl.multiple_of((core * Y + y) * Z, Z), Z)

    def send_group(at, number):
        for low in range(NEAR):
            total = sums[at * Z + low, kept]
            for high in range(1, Z // NEAR):
                total = total + sums[at * Z + high * NEAR + low, kept]
            rows = pl.ds((core * Y + y) * Z + low * KEPT, KEPT)
            for part in range(PARTS):
                panel_ref[at, lag * PARTS + part, rows, :] = total[
                    part * KEPT : (part + 1) * KEPT
                ]
        group_tiles = panel_ref.at[at, lag_tiles, group_rows]
        for y_step in range(Y):
            for step in range(LAG_PARTS):
                if y_step or step:
                    copy(
                        group_tiles,
                        group_tiles,
                        number,
                        chan=owner((y + y_step) % Y, z, core),
                        lag=(lag + step) % LAG_PARTS,
                    ).start()

    seven_sums = sums.at[pl.ds(0, Z - 1), kept]
    eight_sums = sums.at[pl.ds(0, Z), kept]
    wait_all(seven_sums, 3)
    send_group(segment, 7)
    wait_all(eight_sums, 15)
    send_group(1 - segment, 16)

    for part in range(PARTS):
        swaps[part].wait_recv()
        forward(other_tile + part, 13 + part)

    xy_tiles = panel_ref.at[0, pl.ds(0, 5), pl.ds(0, 6 * Z)]
    wait_all(xy_tiles, 7)
    wait_all(xy_tiles, 16)
    core_rows = pl.ds(pl.multiple_of(core * Y * Z, Y * Z), Y * Z)
    half_panel = panel_ref.at[:, :, core_rows]
    across = copy(half_panel, half_panel, 8, chan=owner(y, z, 1 - core))
    across.start()
    three = series_ref.at[pl.ds(0, LAG_PARTS - 1)]
    for number in range(11, 15):
        wait_all(three, number)
    across.wait()
    wait_sent(near_others, 0)
    wait_sent(seven_sums, 3)
    wait_sent(eight_sums, 15)
    for part in range(PARTS):
        wait_sent(seven_plane[part], 1 + part)
        wait_sent(seven_line, 4 + part)
    wait_sent(xy_tiles, 7)
    wait_sent(xy_tiles, 16)
    for number in range(11, 15):
        wait_sent(three, number)

    for part in range(PARTS):
        swaps[part].wait_send()


def correlate(series_ref, panel_ref, out_ref, windows_high, windows_low, shifts_high, shifts_low):
    lag_width = LAGS // LAG_PARTS
    rows = series_ref.shape[1]
    groups = lag_width // COLUMN_LAGS
    start = lax.axis_index("lag") * lag_width
    per_segment = TILES // SEGMENTS
    panel = jnp.concatenate(
        [panel_ref[tile // per_segment, tile % per_segment] for tile in range(TERMS // LANES)]
        + [jnp.zeros((REF, LANES), jnp.float32)] * (TILES - TERMS // LANES),
        axis=1,
    )
    panel = pltpu.roll(panel, start, 1)
    for shift in range(COLUMN_LAGS):
        high, low = split(pltpu.roll(panel, shift, 1) if shift else panel)
        shifts_high[pl.ds(shift * REF, REF), :] = high
        shifts_low[pl.ds(shift * REF, REF), :] = low
    series = jnp.concatenate([series_ref[tile] for tile in range(TILES)], axis=1)
    for group in range(groups):
        lag = group * COLUMN_LAGS
        high, low = split(pltpu.roll(series, SAMPLES - lag, 1) if lag else series)
        windows_high[pl.ds(group * rows, rows), :] = high
        windows_low[pl.ds(group * rows, rows), :] = low
    total = (
        transposed_dot(windows_high[...], shifts_high[...])
        + transposed_dot(windows_high[...], shifts_low[...])
        + transposed_dot(windows_low[...], shifts_high[...])
    )
    width = COLUMN_LAGS * REF
    for group in range(groups):
        out_ref[:, pl.ds(group * width, width)] = total[group * rows : (group + 1) * rows] * (
            1.0 / math.sqrt(TERMS)
        )


VMEM = pl.BlockSpec(memory_space=pltpu.VMEM)


def shards(records_owned, section_list, ref_index):
    series, panel = pl.pallas_call(
        exchange,
        out_shape=[
            jax.ShapeDtypeStruct((TILES, HALF, LANES), jnp.float32),
            jax.ShapeDtypeStruct((SEGMENTS, TILES // SEGMENTS, REF, LANES), jnp.float32),
        ],
        in_specs=[pl.BlockSpec(memory_space=pltpu.HBM)] * 3,
        out_specs=[VMEM] * 2,
        scratch_shapes=[
            pltpu.VMEM((ROWS * PARTS, LANES), jnp.float32),
            pltpu.VMEM((OWNERS, ROWS), jnp.int32),
            pltpu.VMEM((1, REF), jnp.int32),
            pltpu.VMEM((WIDE * NEAR, 8, LANES), jnp.float32),
            pltpu.VMEM((WIDE * NEAR, 8, LANES), jnp.float32),
            pltpu.VMEM((PARTS, WIDE, 2 * Z, LANES), jnp.float32),
            pltpu.VMEM((PARTS, WIDE, 2 * Z, LANES), jnp.float32),
            pltpu.VMEM((PARTS, Z, 2 * WIDE, LANES), jnp.float32),
            pltpu.VMEM((PARTS, Z, 2 * WIDE, LANES), jnp.float32),
            pltpu.VMEM((SEGMENTS * Z, 8, LANES), jnp.float32),
            pltpu.VMEM((PARTS, HALF, LANES), jnp.float32),
            pltpu.SemaphoreType.REGULAR,
            pltpu.SemaphoreType.DMA((3,)),
            pltpu.SemaphoreType.DMA((17,)),
            pltpu.SemaphoreType.DMA((17,)),
        ],
        compiler_params=pltpu.CompilerParams(
            collective_id=0, has_side_effects=True, vmem_limit_bytes=32 * 1024 * 1024
        ),
        name="exchange",
    )(
        *[
            pltpu.with_memory_space_constraint(value, pltpu.HBM)
            for value in (
                records_owned.reshape(ROWS * PARTS, LANES),
                section_list.reshape(OWNERS, ROWS),
                ref_index.reshape(1, REF),
            )
        ]
    )
    lag_width = LAGS // LAG_PARTS
    groups = lag_width // COLUMN_LAGS
    return pl.pallas_call(
        correlate,
        out_shape=jax.ShapeDtypeStruct((HALF, lag_width * REF), jnp.float32),
        in_specs=[VMEM] * 2,
        out_specs=VMEM,
        scratch_shapes=[pltpu.VMEM((groups * HALF, SAMPLES), jnp.bfloat16)] * 2
        + [pltpu.VMEM((COLUMN_LAGS * REF, SAMPLES), jnp.bfloat16)] * 2,
        compiler_params=pltpu.CompilerParams(vmem_limit_bytes=32 * 1024 * 1024),
        name="correlate",
    )(series, panel)


def solution(mesh):
    return jax.shard_map(
        shards,
        mesh=mesh,
        in_specs=(P("chan", "seg", "lag"), P(), P()),
        out_specs=P(("chan", "seg"), "lag"),
        check_vma=False,
    )
```

```python
import math

import jax
import jax.numpy as jnp
from jax import lax
from jax.experimental import pallas as pl
from jax.experimental.pallas import tpu as pltpu
from jax.sharding import PartitionSpec as P

MESH = pl.DeviceIdType.MESH
LAGS = 128
SAMPLES = 2048
REF = 64
TERMS = SAMPLES - LAGS
LANES = 128
TILES = SAMPLES // LANES
COLUMN_LAGS = 4
OWNERS = 64
ROWS = 128
HALF = 64
SEGMENTS = 2
LAG_PARTS = 4
Y, Z, CORES = 4, 8, 2
WIDE = Y * CORES
NEAR = 4
KEPT = Z // NEAR
PARTS = 2


def split(value):
    high = value.astype(jnp.bfloat16)
    return high, (value - high.astype(jnp.float32)).astype(jnp.bfloat16)


def transposed_dot(left, right):
    return lax.dot_general(
        left, right, (((1,), (1,)), ((), ())), preferred_element_type=jnp.float32
    )


def select_rows(chosen, values):
    one_hot = jnp.where(chosen, 1.0, 0.0).astype(jnp.bfloat16)
    high, low = split(values)
    return jnp.dot(one_hot, high, preferred_element_type=jnp.float32) + jnp.dot(
        one_hot, low, preferred_element_type=jnp.float32
    )


def iota(shape, dimension):
    return lax.broadcasted_iota(jnp.int32, shape, dimension)


def exchange(
    records_hbm,
    lists_hbm,
    refs_hbm,
    series_ref,
    panel_ref,
    records_ref,
    lists_ref,
    refs_ref,
    panel_out,
    panel_in,
    outgoing,
    across_plane,
    line_out,
    along_line,
    sums,
    theirs,
    late_sem,
    load_sems,
    send_sems,
    recv_sems,
):
    me = lax.axis_index("chan")
    lag = lax.axis_index("lag")
    segment = lax.axis_index("seg")
    core = me % CORES
    z = (me // CORES) % Z
    y = me // (CORES * Z)
    along = segment * Z + z

    def owner(y_at, z_at, core_at):
        return (y_at * Z + z_at) * CORES + core_at

    wide = y * CORES + core

    def plane_peer(step):
        at = (wide + step) % WIDE
        return owner(at // CORES, z, at % CORES)

    first_near = z // NEAR * NEAR
    near = wide * NEAR + z % NEAR

    def near_peer(step):
        at = (near + step) % (WIDE * NEAR)
        at_wide = at // NEAR
        return at, owner(at_wide // CORES, first_near + at % NEAR, at_wide % CORES)

    def copy(source, target, number, **device):
        return pltpu.make_async_remote_copy(
            src_ref=source,
            dst_ref=target,
            send_sem=send_sems.at[number],
            recv_sem=recv_sems.at[number],
            device_id=device,
            device_id_type=MESH,
        )

    def greet(**device):
        pl.semaphore_signal(barrier, inc=1, device_id=device, device_id_type=MESH)

    def wait_all(block, number):
        copy(block, block, number, lag=(lag + 1) % LAG_PARTS).wait_recv()

    def wait_sent(block, number):
        copy(block, block, number, lag=(lag + 1) % LAG_PARTS).wait_send()

    barrier = pltpu.get_barrier_semaphore()

    loads = [
        pltpu.make_async_copy(source, target, load_sems.at[number])
        for number, (source, target) in enumerate(
            [(records_hbm, records_ref), (lists_hbm, lists_ref), (refs_hbm, refs_ref)]
        )
    ]
    for load in loads:
        load.start()

    @pl.when(segment == 0)
    def _():
        for step in range(Z):
            greet(chan=owner(y, step, core), seg=1)

    for step in range(1, Z // NEAR):
        for at in range(NEAR):
            greet(chan=owner(y, (first_near + step * NEAR + at) % Z, core))
    for y_step in range(Y):
        for step in range(1, LAG_PARTS):
            greet(chan=owner((y + y_step) % Y, z, core), lag=(lag + step) % LAG_PARTS)
    for step in range(1, WIDE * NEAR):
        greet(chan=near_peer(step)[1])
    for load in loads:
        load.wait()

    own = lists_ref[pl.ds(me, 1), :]
    own_down = jnp.transpose(jnp.broadcast_to(own.astype(jnp.float32), (ROWS, ROWS)))
    own_down = own_down.astype(jnp.int32)
    own_block = own // ROWS
    behind = (own_down // ROWS == own_block) & (own_down < own)
    rank = jnp.sum(jnp.where(behind, 1, 0), axis=0, keepdims=True)
    refs = refs_ref[...].astype(jnp.float32)
    refs_down = jnp.transpose(
        jnp.broadcast_to(jnp.concatenate([refs, refs], axis=1), (ROWS, ROWS))
    )[:REF].astype(jnp.int32)
    number = iota((REF, ROWS), 0)
    target = (number // (Y * Z) + (number // Z) % Y * CORES) * NEAR + number % Z // KEPT
    panel_at = jnp.sum(
        jnp.where(refs_down == own, target * 8 + number % KEPT + 1, 0), axis=0, keepdims=True
    )
    panel_at = panel_at - 1
    own_wide = own_block // (Z * CORES) * CORES + own_block % CORES
    series_at = (own_wide * Z + own_block // CORES % Z) * 2 + rank
    series_at = jnp.concatenate([series_at, series_at + ROWS], axis=1)
    panel_at = jnp.concatenate([panel_at, jnp.where(panel_at < 0, -1, panel_at + KEPT)], axis=1)
    place = iota((PARTS * ROWS, PARTS * ROWS), 0)
    panel_place = iota((WIDE * NEAR * 8, PARTS * ROWS), 0)
    records = jnp.concatenate(
        [records_ref[pl.ds(part, ROWS, PARTS), :] for part in range(PARTS)], axis=0
    )
    panel_out[...] = select_rows(panel_place == panel_at, records).reshape(WIDE * NEAR, 8, LANES)
    outgoing[...] = select_rows(place == series_at, records).reshape(PARTS, WIDE, 2 * Z, LANES)

    pl.semaphore_wait(barrier, WIDE * NEAR - 1 + Z - NEAR + Y * (LAG_PARTS - 1) + Z * segment)

    for part in range(PARTS):
        for step in range(1, WIDE):
            at = (wide + step) % WIDE
            copy(
                outgoing.at[part, at],
                across_plane.at[part, wide],
                1 + part,
                chan=plane_peer(step),
            ).start()
        across_plane[part, wide] = outgoing[part, wide]

    kept = pl.ds(0, PARTS * KEPT)
    for step in range(1, WIDE * NEAR):
        at, peer = near_peer(step)
        copy(panel_out.at[at, kept], panel_in.at[near, kept], 0, chan=peer).start()
    panel_in[near] = panel_out[near]

    @pl.when(segment == 1)
    def _():
        for step in range(Z):
            pl.semaphore_signal(
                late_sem,
                inc=1,
                device_id={"chan": owner(y, step, core), "seg": 0},
                device_id_type=MESH,
            )

    lists = lists_ref[...].astype(jnp.float32)
    lists = jnp.transpose(jnp.concatenate([lists, lists], axis=0)).astype(jnp.int32)
    inside = lists // ROWS == me
    first = jnp.min(jnp.where(inside, lists, OWNERS * ROWS), axis=0, keepdims=True)
    second = jnp.max(jnp.where(inside, lists, -1), axis=0, keepdims=True)
    ids = jnp.where(iota((1, ROWS), 1) < OWNERS, first, second)
    turned = me * ROWS + (iota((ROWS, ROWS), 0) + segment * HALF) % ROWS
    down, right = iota((ROWS, ROWS), 0), iota((ROWS, ROWS), 1)
    right_wide = right // 2 % WIDE
    right_owner = owner(right_wide // CORES, right // (2 * WIDE), right_wide % CORES)
    reorder = jnp.where(down == right % 2 * OWNERS + right_owner, 1.0, 0.0).astype(jnp.bfloat16)
    placing = (
        jnp.dot(
            jnp.where(turned == ids, 1.0, 0.0).astype(jnp.bfloat16),
            reorder,
            preferred_element_type=jnp.float32,
        )
        > 0.5
    )
    by_line = right == (down // 2 % WIDE * Z + down // (2 * WIDE)) * 2 + down % 2

    seven_plane = [across_plane.at[part, pl.ds(0, WIDE - 1)] for part in range(PARTS)]
    near_others = panel_in.at[pl.ds(0, WIDE * NEAR - 1), kept]
    seven_line = along_line.at[0, pl.ds(0, Z - 1)]

    def send_line(part):
        wait_all(seven_plane[part], 1 + part)
        line_out[part] = select_rows(
            by_line, across_plane[part].reshape(ROWS, LANES)
        ).reshape(Z, 2 * WIDE, LANES)
        for step in range(1, Z):
            at = (z + step) % Z
            copy(
                line_out.at[part, at], along_line.at[part, z], 4 + part, chan=owner(y, at, core)
            ).start()
        along_line[part, z] = line_out[part, z]

    send_line(0)
    wait_all(near_others, 0)
    sums[along, kept] = jnp.sum(panel_in[:, kept], axis=0)
    for step in range(1, Z):
        copy(
            sums.at[along, kept], sums.at[along, kept], 3, chan=owner(y, (z + step) % Z, core)
        ).start()

    def send_sums_over():
        for step in range(Z):
            copy(
                sums.at[along, kept],
                sums.at[along, kept],
                15,
                chan=owner(y, (z + step) % Z, core),
                seg=1 - segment,
            ).start()

    @pl.when(segment == 1)
    def _():
        send_sums_over()

    send_line(1)

    own_tile = (segment * LAG_PARTS + lag) * PARTS
    other_tile = ((1 - segment) * LAG_PARTS + lag) * PARTS
    swaps = [
        copy(theirs.at[part], series_ref.at[own_tile + part], 9 + part, seg=1 - segment)
        for part in range(PARTS)
    ]

    def forward(tile, number):
        for step in range(1, LAG_PARTS):
            copy(
                series_ref.at[tile], series_ref.at[tile], number, lag=(lag + step) % LAG_PARTS
            ).start()

    def place_part(part):
        wait_all(seven_line, 4 + part)
        placed = select_rows(placing, along_line[part].reshape(ROWS, LANES))
        theirs[part] = placed[HALF:]
        if part == 0:

            @pl.when(segment == 0)
            def _():
                pl.semaphore_wait(late_sem, Z)

            swaps[part].start()
        else:

            @pl.when(segment == 1)
            def _():
                swaps[part].start()

        series_ref[own_tile + part] = placed[:HALF]
        forward(own_tile + part, 11 + part)

    place_part(0)
    place_part(1)

    @pl.when(segment == 0)
    def _():
        send_sums_over()

    lag_tiles = pl.ds(lag * PARTS, PARTS)
    group_rows = pl.ds(pl.multiple_of((core * Y + y) * Z, Z), Z)

    def send_group(at, number):
        for low in range(NEAR):
            total = sums[at * Z + low, kept]
            for high in range(1, Z // NEAR):
                total = total + sums[at * Z + high * NEAR + low, kept]
            rows = pl.ds((core * Y + y) * Z + low * KEPT, KEPT)
            for part in range(PARTS):
                panel_ref[at, lag * PARTS + part, rows, :] = total[
                    part * KEPT : (part + 1) * KEPT
                ]
        group_tiles = panel_ref.at[at, lag_tiles, group_rows]
        for y_step in range(Y):
            for step in range(LAG_PARTS):
                if y_step or step:
                    copy(
                        group_tiles,
                        group_tiles,
                        number,
                        chan=owner((y + y_step) % Y, z, core),
                        lag=(lag + step) % LAG_PARTS,
                    ).start()

    seven_sums = sums.at[pl.ds(0, Z - 1), kept]
    eight_sums = sums.at[pl.ds(0, Z), kept]
    wait_all(seven_sums, 3)
    send_group(segment, 7)
    wait_all(eight_sums, 15)
    send_group(1 - segment, 16)

    for part in range(PARTS):
        swaps[part].wait_recv()
        forward(other_tile + part, 13 + part)
        if part == 0:

            @pl.when(segment == 0)
            def _():
                swaps[1].start()


    xy_tiles = panel_ref.at[0, pl.ds(0, 5), pl.ds(0, 6 * Z)]
    wait_all(xy_tiles, 7)
    wait_all(xy_tiles, 16)
    core_rows = pl.ds(pl.multiple_of(core * Y * Z, Y * Z), Y * Z)
    half_panel = panel_ref.at[:, :, core_rows]
    across = copy(half_panel, half_panel, 8, chan=owner(y, z, 1 - core))
    across.start()
    three = series_ref.at[pl.ds(0, LAG_PARTS - 1)]
    for number in range(11, 15):
        wait_all(three, number)
    across.wait()
    wait_sent(near_others, 0)
    wait_sent(seven_sums, 3)
    wait_sent(eight_sums, 15)
    for part in range(PARTS):
        wait_sent(seven_plane[part], 1 + part)
        wait_sent(seven_line, 4 + part)
    wait_sent(xy_tiles, 7)
    wait_sent(xy_tiles, 16)
    for number in range(11, 15):
        wait_sent(three, number)

    for part in range(PARTS):
        swaps[part].wait_send()


def correlate(series_ref, panel_ref, out_ref, windows_high, windows_low, shifts_high, shifts_low):
    lag_width = LAGS // LAG_PARTS
    rows = series_ref.shape[1]
    groups = lag_width // COLUMN_LAGS
    start = lax.axis_index("lag") * lag_width
    per_segment = TILES // SEGMENTS
    panel = jnp.concatenate(
        [panel_ref[tile // per_segment, tile % per_segment] for tile in range(TERMS // LANES)]
        + [jnp.zeros((REF, LANES), jnp.float32)] * (TILES - TERMS // LANES),
        axis=1,
    )
    panel = pltpu.roll(panel, start, 1)
    for shift in range(COLUMN_LAGS):
        high, low = split(pltpu.roll(panel, shift, 1) if shift else panel)
        shifts_high[pl.ds(shift * REF, REF), :] = high
        shifts_low[pl.ds(shift * REF, REF), :] = low
    series = jnp.concatenate([series_ref[tile] for tile in range(TILES)], axis=1)
    for group in range(groups):
        lag = group * COLUMN_LAGS
        high, low = split(pltpu.roll(series, SAMPLES - lag, 1) if lag else series)
        windows_high[pl.ds(group * rows, rows), :] = high
        windows_low[pl.ds(group * rows, rows), :] = low
    total = (
        transposed_dot(windows_high[...], shifts_high[...])
        + transposed_dot(windows_high[...], shifts_low[...])
        + transposed_dot(windows_low[...], shifts_high[...])
    )
    width = COLUMN_LAGS * REF
    for group in range(groups):
        out_ref[:, pl.ds(group * width, width)] = total[group * rows : (group + 1) * rows] * (
            1.0 / math.sqrt(TERMS)
        )


VMEM = pl.BlockSpec(memory_space=pltpu.VMEM)


def shards(records_owned, section_list, ref_index):
    series, panel = pl.pallas_call(
        exchange,
        out_shape=[
            jax.ShapeDtypeStruct((TILES, HALF, LANES), jnp.float32),
            jax.ShapeDtypeStruct((SEGMENTS, TILES // SEGMENTS, REF, LANES), jnp.float32),
        ],
        in_specs=[pl.BlockSpec(memory_space=pltpu.HBM)] * 3,
        out_specs=[VMEM] * 2,
        scratch_shapes=[
            pltpu.VMEM((ROWS * PARTS, LANES), jnp.float32),
            pltpu.VMEM((OWNERS, ROWS), jnp.int32),
            pltpu.VMEM((1, REF), jnp.int32),
            pltpu.VMEM((WIDE * NEAR, 8, LANES), jnp.float32),
            pltpu.VMEM((WIDE * NEAR, 8, LANES), jnp.float32),
            pltpu.VMEM((PARTS, WIDE, 2 * Z, LANES), jnp.float32),
            pltpu.VMEM((PARTS, WIDE, 2 * Z, LANES), jnp.float32),
            pltpu.VMEM((PARTS, Z, 2 * WIDE, LANES), jnp.float32),
            pltpu.VMEM((PARTS, Z, 2 * WIDE, LANES), jnp.float32),
            pltpu.VMEM((SEGMENTS * Z, 8, LANES), jnp.float32),
            pltpu.VMEM((PARTS, HALF, LANES), jnp.float32),
            pltpu.SemaphoreType.REGULAR,
            pltpu.SemaphoreType.DMA((3,)),
            pltpu.SemaphoreType.DMA((17,)),
            pltpu.SemaphoreType.DMA((17,)),
        ],
        compiler_params=pltpu.CompilerParams(
            collective_id=0, has_side_effects=True, vmem_limit_bytes=32 * 1024 * 1024
        ),
        name="exchange",
    )(
        *[
            pltpu.with_memory_space_constraint(value, pltpu.HBM)
            for value in (
                records_owned.reshape(ROWS * PARTS, LANES),
                section_list.reshape(OWNERS, ROWS),
                ref_index.reshape(1, REF),
            )
        ]
    )
    lag_width = LAGS // LAG_PARTS
    groups = lag_width // COLUMN_LAGS
    return pl.pallas_call(
        correlate,
        out_shape=jax.ShapeDtypeStruct((HALF, lag_width * REF), jnp.float32),
        in_specs=[VMEM] * 2,
        out_specs=VMEM,
        scratch_shapes=[pltpu.VMEM((groups * HALF, SAMPLES), jnp.bfloat16)] * 2
        + [pltpu.VMEM((COLUMN_LAGS * REF, SAMPLES), jnp.bfloat16)] * 2,
        compiler_params=pltpu.CompilerParams(vmem_limit_bytes=32 * 1024 * 1024),
        name="correlate",
    )(series, panel)


def solution(mesh):
    return jax.shard_map(
        shards,
        mesh=mesh,
        in_specs=(P("chan", "seg", "lag"), P(), P()),
        out_specs=P(("chan", "seg"), "lag"),
        check_vma=False,
    )
```

```python
import math

import jax
import jax.numpy as jnp
from jax import lax
from jax.experimental import pallas as pl
from jax.experimental.pallas import tpu as pltpu
from jax.sharding import PartitionSpec as P

MESH = pl.DeviceIdType.MESH
LAGS = 128
SAMPLES = 2048
REF = 64
TERMS = SAMPLES - LAGS
LANES = 128
TILES = SAMPLES // LANES
COLUMN_LAGS = 4
OWNERS = 64
ROWS = 128
HALF = 64
SEGMENTS = 2
LAG_PARTS = 4
Y, Z, CORES = 4, 8, 2
WIDE = Y * CORES
NEAR = 4
PIECES = 2
HELD = 1
KEPT = Z // NEAR
PARTS = 2


def split(value):
    high = value.astype(jnp.bfloat16)
    return high, (value - high.astype(jnp.float32)).astype(jnp.bfloat16)


def transposed_dot(left, right):
    return lax.dot_general(
        left, right, (((1,), (1,)), ((), ())), preferred_element_type=jnp.float32
    )


def select_rows(chosen, values):
    one_hot = jnp.where(chosen, 1.0, 0.0).astype(jnp.bfloat16)
    high, low = split(values)
    return jnp.dot(one_hot, high, preferred_element_type=jnp.float32) + jnp.dot(
        one_hot, low, preferred_element_type=jnp.float32
    )


def iota(shape, dimension):
    return lax.broadcasted_iota(jnp.int32, shape, dimension)


def exchange(
    records_hbm,
    lists_hbm,
    refs_hbm,
    series_ref,
    panel_ref,
    records_ref,
    lists_ref,
    refs_ref,
    panel_out,
    panel_in,
    outgoing,
    arrived,
    sums,
    theirs,
    late_sem,
    load_sems,
    send_sems,
    recv_sems,
):
    me = lax.axis_index("chan")
    lag = lax.axis_index("lag")
    segment = lax.axis_index("seg")
    core = me % CORES
    z = (me // CORES) % Z
    y = me // (CORES * Z)
    along = segment * Z + z

    def owner(y_at, z_at, core_at):
        return (y_at * Z + z_at) * CORES + core_at

    wide = y * CORES + core

    first_near = z // NEAR * NEAR
    near = wide * NEAR + z % NEAR

    def near_peer(step):
        at = (near + step) % (WIDE * NEAR)
        at_wide = at // NEAR
        return at, owner(at_wide // CORES, first_near + at % NEAR, at_wide % CORES)

    def copy(source, target, number, **device):
        return pltpu.make_async_remote_copy(
            src_ref=source,
            dst_ref=target,
            send_sem=send_sems.at[number],
            recv_sem=recv_sems.at[number],
            device_id=device,
            device_id_type=MESH,
        )

    def greet(**device):
        pl.semaphore_signal(barrier, inc=1, device_id=device, device_id_type=MESH)

    def wait_all(block, number):
        copy(block, block, number, lag=(lag + 1) % LAG_PARTS).wait_recv()

    def wait_sent(block, number):
        copy(block, block, number, lag=(lag + 1) % LAG_PARTS).wait_send()

    barrier = pltpu.get_barrier_semaphore()

    loads = [
        pltpu.make_async_copy(source, target, load_sems.at[number])
        for number, (source, target) in enumerate(
            [(records_hbm, records_ref), (lists_hbm, lists_ref), (refs_hbm, refs_ref)]
        )
    ]
    for load in loads:
        load.start()

    @pl.when(segment == 0)
    def _():
        for step in range(Z):
            greet(chan=owner(y, step, core), seg=1)

    def greet_owner(step, carry):
        greet(chan=(me + step) % OWNERS)
        return carry

    lax.fori_loop(1, OWNERS, greet_owner, 0)
    for y_step in range(Y):
        for step in range(1, LAG_PARTS):
            greet(chan=owner((y + y_step) % Y, z, core), lag=(lag + step) % LAG_PARTS)
    for load in loads:
        load.wait()

    own = lists_ref[pl.ds(me, 1), :]
    own_down = jnp.transpose(jnp.broadcast_to(own.astype(jnp.float32), (ROWS, ROWS)))
    own_down = own_down.astype(jnp.int32)
    own_block = own // ROWS
    behind = (own_down // ROWS == own_block) & (own_down < own)
    rank = jnp.sum(jnp.where(behind, 1, 0), axis=0, keepdims=True)
    refs = refs_ref[...].astype(jnp.float32)
    refs_down = jnp.transpose(
        jnp.broadcast_to(jnp.concatenate([refs, refs], axis=1), (ROWS, ROWS))
    )[:REF].astype(jnp.int32)
    number = iota((REF, ROWS), 0)
    target = (number // (Y * Z) + (number // Z) % Y * CORES) * NEAR + number % Z // KEPT
    panel_at = jnp.sum(
        jnp.where(refs_down == own, target * 8 + number % KEPT + 1, 0), axis=0, keepdims=True
    )
    panel_at = panel_at - 1
    series_at = own_block * 8 + rank
    series_at = jnp.concatenate([series_at, series_at + 2], axis=1)
    panel_at = jnp.concatenate([panel_at, jnp.where(panel_at < 0, -1, panel_at + KEPT)], axis=1)
    place = iota((OWNERS * 8, PARTS * ROWS), 0)
    panel_place = iota((WIDE * NEAR * 8, PARTS * ROWS), 0)
    records = jnp.concatenate(
        [records_ref[pl.ds(part, ROWS, PARTS), :] for part in range(PARTS)], axis=0
    )
    panel_out[...] = select_rows(panel_place == panel_at, records).reshape(WIDE * NEAR, 8, LANES)
    outgoing[...] = select_rows(place == series_at, records).reshape(OWNERS, 8, LANES)

    pl.semaphore_wait(barrier, OWNERS - 1 + Y * (LAG_PARTS - 1) + Z * segment)

    def send_part(part):
        pair = pl.ds(2 * part, 2)

        def send_owner(step, carry):
            peer = (me + step) % OWNERS
            copy(outgoing.at[peer, pair], arrived.at[me, pair], 1 + part, chan=peer).start()
            return carry

        lax.fori_loop(1, OWNERS, send_owner, 0)

    send_part(0)
    kept = pl.ds(0, PARTS * KEPT)
    for step in range(1, WIDE * NEAR):
        at, peer = near_peer(step)
        copy(panel_out.at[at, kept], panel_in.at[near, kept], 0, chan=peer).start()
    panel_in[near] = panel_out[near]
    send_part(1)
    arrived[me] = outgoing[me]

    @pl.when(segment == 1)
    def _():
        for step in range(Z):
            pl.semaphore_signal(
                late_sem,
                inc=1,
                device_id={"chan": owner(y, step, core), "seg": 0},
                device_id_type=MESH,
            )

    lists = lists_ref[...].astype(jnp.float32)
    lists = jnp.transpose(jnp.concatenate([lists, lists], axis=0)).astype(jnp.int32)
    inside = lists // ROWS == me
    first = jnp.min(jnp.where(inside, lists, OWNERS * ROWS), axis=0, keepdims=True)
    second = jnp.max(jnp.where(inside, lists, -1), axis=0, keepdims=True)
    ids = jnp.where(iota((1, ROWS), 1) < OWNERS, first, second)
    turned = me * ROWS + (iota((ROWS, ROWS), 0) + segment * HALF) % ROWS
    placing = turned == ids
    others = [arrived.at[pl.ds(0, OWNERS - 1), pl.ds(2 * part, 2)] for part in range(PARTS)]
    near_others = panel_in.at[pl.ds(0, WIDE * NEAR - 1), kept]

    wait_all(near_others, 0)
    sums[along, kept] = jnp.sum(panel_in[:, kept], axis=0)
    for step in range(1, Z):
        copy(
            sums.at[along, kept], sums.at[along, kept], 3, chan=owner(y, (z + step) % Z, core)
        ).start()

    def send_sums_over():
        for step in range(Z):
            copy(
                sums.at[along, kept],
                sums.at[along, kept],
                15,
                chan=owner(y, (z + step) % Z, core),
                seg=1 - segment,
            ).start()

    @pl.when(segment == 1)
    def _():
        send_sums_over()


    own_tile = (segment * LAG_PARTS + lag) * PARTS
    other_tile = ((1 - segment) * LAG_PARTS + lag) * PARTS
    pieces = [
        (part, pl.ds(piece * HALF // PIECES, HALF // PIECES))
        for part in range(PARTS)
        for piece in range(PIECES)
    ]
    swaps = [
        copy(theirs.at[part, rows], series_ref.at[own_tile + part, rows], 17 + at, seg=1 - segment)
        for at, (part, rows) in enumerate(pieces)
    ]

    def forward(tile, number, rows=pl.ds(0, HALF)):
        block = series_ref.at[tile, rows]
        for step in range(1, LAG_PARTS):
            copy(block, block, number, lag=(lag + step) % LAG_PARTS).start()

    def place_part(part):
        wait_all(others[part], 1 + part)
        placed = select_rows(
            placing,
            jnp.concatenate([arrived[:, 2 * part + slot, :] for slot in range(2)], axis=0),
        )
        theirs[part] = placed[HALF:]

        def start_swaps():
            for at, (piece_part, _) in enumerate(pieces):
                if piece_part == part:
                    swaps[at].start()

        if part == 0:

            @pl.when(segment == 0)
            def _():
                pl.semaphore_wait(late_sem, Z)

            start_swaps()
        else:
            pl.when(segment == 1)(start_swaps)

        series_ref[own_tile + part] = placed[:HALF]
        forward(own_tile + part, 11 + part)

    place_part(0)
    place_part(1)

    @pl.when(segment == 0)
    def _():
        send_sums_over()

    lag_tiles = pl.ds(lag * PARTS, PARTS)
    group_rows = pl.ds(pl.multiple_of((core * Y + y) * Z, Z), Z)

    def send_group(at, number):
        for low in range(NEAR):
            total = sums[at * Z + low, kept]
            for high in range(1, Z // NEAR):
                total = total + sums[at * Z + high * NEAR + low, kept]
            rows = pl.ds((core * Y + y) * Z + low * KEPT, KEPT)
            for part in range(PARTS):
                panel_ref[at, lag * PARTS + part, rows, :] = total[
                    part * KEPT : (part + 1) * KEPT
                ]
        group_tiles = panel_ref.at[at, lag_tiles, group_rows]
        for y_step in range(Y):
            for step in range(LAG_PARTS):
                if y_step or step:
                    copy(
                        group_tiles,
                        group_tiles,
                        number,
                        chan=owner((y + y_step) % Y, z, core),
                        lag=(lag + step) % LAG_PARTS,
                    ).start()

    seven_sums = sums.at[pl.ds(0, Z - 1), kept]
    eight_sums = sums.at[pl.ds(0, Z), kept]
    wait_all(seven_sums, 3)
    send_group(segment, 7)
    wait_all(eight_sums, 15)
    send_group(1 - segment, 16)

    for at, (part, rows) in enumerate(pieces):
        swaps[at].wait_recv()
        forward(other_tile + part, 17 + len(pieces) + at, rows)
        if at == HELD:

            @pl.when(segment == 0)
            def _():
                for swap in swaps[PIECES:]:
                    swap.start()

    xy_tiles = panel_ref.at[0, pl.ds(0, 5), pl.ds(0, 6 * Z)]
    wait_all(xy_tiles, 7)
    wait_all(xy_tiles, 16)
    core_rows = pl.ds(pl.multiple_of(core * Y * Z, Y * Z), Y * Z)
    half_panel = panel_ref.at[:, :, core_rows]
    across = copy(half_panel, half_panel, 8, chan=owner(y, z, 1 - core))
    across.start()
    three = series_ref.at[pl.ds(0, LAG_PARTS - 1)]
    for number in (11, 12):
        wait_all(three, number)
    three_pieces = series_ref.at[pl.ds(0, LAG_PARTS - 1), pl.ds(0, HALF // PIECES)]
    for at in range(len(pieces)):
        wait_all(three_pieces, 17 + len(pieces) + at)
    across.wait()
    wait_sent(near_others, 0)
    wait_sent(seven_sums, 3)
    wait_sent(eight_sums, 15)
    for part in range(PARTS):
        wait_sent(others[part], 1 + part)
    wait_sent(xy_tiles, 7)
    wait_sent(xy_tiles, 16)
    for number in (11, 12):
        wait_sent(three, number)
    for at in range(len(pieces)):
        wait_sent(three_pieces, 17 + len(pieces) + at)
    for swap in swaps:
        swap.wait_send()


def correlate(series_ref, panel_ref, out_ref, windows_high, windows_low, shifts_high, shifts_low):
    lag_width = LAGS // LAG_PARTS
    rows = series_ref.shape[1]
    groups = lag_width // COLUMN_LAGS
    start = lax.axis_index("lag") * lag_width
    per_segment = TILES // SEGMENTS
    panel = jnp.concatenate(
        [panel_ref[tile // per_segment, tile % per_segment] for tile in range(TERMS // LANES)]
        + [jnp.zeros((REF, LANES), jnp.float32)] * (TILES - TERMS // LANES),
        axis=1,
    )
    panel = pltpu.roll(panel, start, 1)
    for shift in range(COLUMN_LAGS):
        high, low = split(pltpu.roll(panel, shift, 1) if shift else panel)
        shifts_high[pl.ds(shift * REF, REF), :] = high
        shifts_low[pl.ds(shift * REF, REF), :] = low
    series = jnp.concatenate([series_ref[tile] for tile in range(TILES)], axis=1)
    for group in range(groups):
        lag = group * COLUMN_LAGS
        high, low = split(pltpu.roll(series, SAMPLES - lag, 1) if lag else series)
        windows_high[pl.ds(group * rows, rows), :] = high
        windows_low[pl.ds(group * rows, rows), :] = low
    total = (
        transposed_dot(windows_high[...], shifts_high[...])
        + transposed_dot(windows_high[...], shifts_low[...])
        + transposed_dot(windows_low[...], shifts_high[...])
    )
    width = COLUMN_LAGS * REF
    for group in range(groups):
        out_ref[:, pl.ds(group * width, width)] = total[group * rows : (group + 1) * rows] * (
            1.0 / math.sqrt(TERMS)
        )


VMEM = pl.BlockSpec(memory_space=pltpu.VMEM)


def shards(records_owned, section_list, ref_index):
    series, panel = pl.pallas_call(
        exchange,
        out_shape=[
            jax.ShapeDtypeStruct((TILES, HALF, LANES), jnp.float32),
            jax.ShapeDtypeStruct((SEGMENTS, TILES // SEGMENTS, REF, LANES), jnp.float32),
        ],
        in_specs=[pl.BlockSpec(memory_space=pltpu.HBM)] * 3,
        out_specs=[VMEM] * 2,
        scratch_shapes=[
            pltpu.VMEM((ROWS * PARTS, LANES), jnp.float32),
            pltpu.VMEM((OWNERS, ROWS), jnp.int32),
            pltpu.VMEM((1, REF), jnp.int32),
            pltpu.VMEM((WIDE * NEAR, 8, LANES), jnp.float32),
            pltpu.VMEM((WIDE * NEAR, 8, LANES), jnp.float32),
            pltpu.VMEM((OWNERS, 8, LANES), jnp.float32),
            pltpu.VMEM((OWNERS, 8, LANES), jnp.float32),
            pltpu.VMEM((SEGMENTS * Z, 8, LANES), jnp.float32),
            pltpu.VMEM((PARTS, HALF, LANES), jnp.float32),
            pltpu.SemaphoreType.REGULAR,
            pltpu.SemaphoreType.DMA((3,)),
            pltpu.SemaphoreType.DMA((25,)),
            pltpu.SemaphoreType.DMA((25,)),
        ],
        compiler_params=pltpu.CompilerParams(
            collective_id=0, has_side_effects=True, vmem_limit_bytes=32 * 1024 * 1024
        ),
        name="exchange",
    )(
        *[
            pltpu.with_memory_space_constraint(value, pltpu.HBM)
            for value in (
                records_owned.reshape(ROWS * PARTS, LANES),
                section_list.reshape(OWNERS, ROWS),
                ref_index.reshape(1, REF),
            )
        ]
    )
    lag_width = LAGS // LAG_PARTS
    groups = lag_width // COLUMN_LAGS
    return pl.pallas_call(
        correlate,
        out_shape=jax.ShapeDtypeStruct((HALF, lag_width * REF), jnp.float32),
        in_specs=[VMEM] * 2,
        out_specs=VMEM,
        scratch_shapes=[pltpu.VMEM((groups * HALF, SAMPLES), jnp.bfloat16)] * 2
        + [pltpu.VMEM((COLUMN_LAGS * REF, SAMPLES), jnp.bfloat16)] * 2,
        compiler_params=pltpu.CompilerParams(vmem_limit_bytes=32 * 1024 * 1024),
        name="correlate",
    )(series, panel)


def solution(mesh):
    return jax.shard_map(
        shards,
        mesh=mesh,
        in_specs=(P("chan", "seg", "lag"), P(), P()),
        out_specs=P(("chan", "seg"), "lag"),
        check_vma=False,
    )
```

```python
import math

import jax
import jax.numpy as jnp
from jax import lax
from jax.experimental import pallas as pl
from jax.experimental.pallas import tpu as pltpu
from jax.sharding import PartitionSpec as P

MESH = pl.DeviceIdType.MESH
LAGS = 128
SAMPLES = 2048
REF = 64
TERMS = SAMPLES - LAGS
LANES = 128
TILES = SAMPLES // LANES
COLUMN_LAGS = 4
OWNERS = 64
ROWS = 128
HALF = 64
SEGMENTS = 2
LAG_PARTS = 4
Y, Z, CORES = 4, 8, 2
WIDE = Y * CORES
NEAR = 4
PIECES = 2
HELD = 1
KEPT = Z // NEAR
PARTS = 2


def split(value):
    high = value.astype(jnp.bfloat16)
    return high, (value - high.astype(jnp.float32)).astype(jnp.bfloat16)


def transposed_dot(left, right):
    return lax.dot_general(
        left, right, (((1,), (1,)), ((), ())), preferred_element_type=jnp.float32
    )


def select_rows(chosen, values):
    one_hot = jnp.where(chosen, 1.0, 0.0).astype(jnp.bfloat16)
    high, low = split(values)
    return jnp.dot(one_hot, high, preferred_element_type=jnp.float32) + jnp.dot(
        one_hot, low, preferred_element_type=jnp.float32
    )


def iota(shape, dimension):
    return lax.broadcasted_iota(jnp.int32, shape, dimension)


def exchange(
    records_hbm,
    lists_hbm,
    refs_hbm,
    series_ref,
    panel_ref,
    records_ref,
    lists_ref,
    refs_ref,
    panel_out,
    panel_in,
    outgoing,
    arrived,
    sums,
    theirs,
    late_sem,
    load_sems,
    send_sems,
    recv_sems,
):
    me = lax.axis_index("chan")
    lag = lax.axis_index("lag")
    segment = lax.axis_index("seg")
    core = me % CORES
    z = (me // CORES) % Z
    y = me // (CORES * Z)
    along = segment * Z + z

    def owner(y_at, z_at, core_at):
        return (y_at * Z + z_at) * CORES + core_at

    wide = y * CORES + core

    first_near = z // NEAR * NEAR
    near = wide * NEAR + z % NEAR

    def near_peer(step):
        at = (near + step) % (WIDE * NEAR)
        at_wide = at // NEAR
        return at, owner(at_wide // CORES, first_near + at % NEAR, at_wide % CORES)

    def copy(source, target, number, **device):
        return pltpu.make_async_remote_copy(
            src_ref=source,
            dst_ref=target,
            send_sem=send_sems.at[number],
            recv_sem=recv_sems.at[number],
            device_id=device,
            device_id_type=MESH,
        )

    def greet(**device):
        pl.semaphore_signal(barrier, inc=1, device_id=device, device_id_type=MESH)

    def wait_all(block, number):
        copy(block, block, number, lag=(lag + 1) % LAG_PARTS).wait_recv()

    def wait_sent(block, number):
        copy(block, block, number, lag=(lag + 1) % LAG_PARTS).wait_send()

    barrier = pltpu.get_barrier_semaphore()

    loads = [
        pltpu.make_async_copy(source, target, load_sems.at[number])
        for number, (source, target) in enumerate(
            [(records_hbm, records_ref), (lists_hbm, lists_ref), (refs_hbm, refs_ref)]
        )
    ]
    for load in loads:
        load.start()

    @pl.when(segment == 0)
    def _():
        for step in range(Z):
            greet(chan=owner(y, step, core), seg=1)

    def greet_owner(step, carry):
        greet(chan=(me + step) % OWNERS)
        return carry

    lax.fori_loop(1, OWNERS, greet_owner, 0)
    for y_step in range(Y):
        for step in range(1, LAG_PARTS):
            greet(chan=owner((y + y_step) % Y, z, core), lag=(lag + step) % LAG_PARTS)
    for load in loads:
        load.wait()

    own = lists_ref[pl.ds(me, 1), :]
    own_down = jnp.transpose(jnp.broadcast_to(own.astype(jnp.float32), (ROWS, ROWS)))
    own_down = own_down.astype(jnp.int32)
    own_block = own // ROWS
    behind = (own_down // ROWS == own_block) & (own_down < own)
    rank = jnp.sum(jnp.where(behind, 1, 0), axis=0, keepdims=True)
    refs = refs_ref[...].astype(jnp.float32)
    refs_down = jnp.transpose(
        jnp.broadcast_to(jnp.concatenate([refs, refs], axis=1), (ROWS, ROWS))
    )[:REF].astype(jnp.int32)
    number = iota((REF, ROWS), 0)
    target = (number // (Y * Z) + (number // Z) % Y * CORES) * NEAR + number % Z // KEPT
    panel_at = jnp.sum(
        jnp.where(refs_down == own, target * 8 + number % KEPT + 1, 0), axis=0, keepdims=True
    )
    panel_at = panel_at - 1
    series_at = own_block * 8 + rank
    series_at = jnp.concatenate([series_at, series_at + 2], axis=1)
    panel_at = jnp.concatenate([panel_at, jnp.where(panel_at < 0, -1, panel_at + KEPT)], axis=1)
    place = iota((OWNERS * 8, PARTS * ROWS), 0)
    panel_place = iota((WIDE * NEAR * 8, PARTS * ROWS), 0)
    records = jnp.concatenate(
        [records_ref[pl.ds(part, ROWS, PARTS), :] for part in range(PARTS)], axis=0
    )
    panel_out[...] = select_rows(panel_place == panel_at, records).reshape(WIDE * NEAR, 8, LANES)
    outgoing[...] = select_rows(place == series_at, records).reshape(OWNERS, 8, LANES)

    pl.semaphore_wait(barrier, OWNERS - 1 + Y * (LAG_PARTS - 1) + Z * segment)

    def send_part(part):
        pair = pl.ds(2 * part, 2)

        def send_owner(step, carry):
            peer = (me + step) % OWNERS
            copy(outgoing.at[peer, pair], arrived.at[me, pair], 1 + part, chan=peer).start()
            return carry

        lax.fori_loop(1, OWNERS, send_owner, 0)

    send_part(0)
    kept = pl.ds(0, PARTS * KEPT)
    for step in range(1, WIDE * NEAR):
        at, peer = near_peer(step)
        copy(panel_out.at[at, kept], panel_in.at[near, kept], 0, chan=peer).start()
    panel_in[near] = panel_out[near]
    send_part(1)
    arrived[me] = outgoing[me]

    @pl.when(segment == 1)
    def _():
        for step in range(Z):
            pl.semaphore_signal(
                late_sem,
                inc=1,
                device_id={"chan": owner(y, step, core), "seg": 0},
                device_id_type=MESH,
            )

    lists = lists_ref[...].astype(jnp.float32)
    lists = jnp.transpose(jnp.concatenate([lists, lists], axis=0)).astype(jnp.int32)
    inside = lists // ROWS == me
    first = jnp.min(jnp.where(inside, lists, OWNERS * ROWS), axis=0, keepdims=True)
    second = jnp.max(jnp.where(inside, lists, -1), axis=0, keepdims=True)
    ids = jnp.where(iota((1, ROWS), 1) < OWNERS, first, second)
    turned = me * ROWS + (iota((ROWS, ROWS), 0) + segment * HALF) % ROWS
    placing = turned == ids
    others = [arrived.at[pl.ds(0, OWNERS - 1), pl.ds(2 * part, 2)] for part in range(PARTS)]
    near_others = panel_in.at[pl.ds(0, WIDE * NEAR - 1), kept]

    wait_all(near_others, 0)
    sums[along, kept] = jnp.sum(panel_in[:, kept], axis=0)
    for step in range(1, Z):
        copy(
            sums.at[along, kept], sums.at[along, kept], 3, chan=owner(y, (z + step) % Z, core)
        ).start()

    def send_sums_over():
        for step in range(Z):
            copy(
                sums.at[along, kept],
                sums.at[along, kept],
                15,
                chan=owner(y, (z + step) % Z, core),
                seg=1 - segment,
            ).start()

    @pl.when(segment == 1)
    def _():
        send_sums_over()


    own_tile = (segment * LAG_PARTS + lag) * PARTS
    other_tile = ((1 - segment) * LAG_PARTS + lag) * PARTS
    pieces = [
        (part, pl.ds(piece * HALF // PIECES, HALF // PIECES))
        for part in range(PARTS)
        for piece in range(PIECES)
    ]
    swaps = [
        copy(theirs.at[part, rows], series_ref.at[own_tile + part, rows], 17 + at, seg=1 - segment)
        for at, (part, rows) in enumerate(pieces)
    ]

    def forward(tile, number, rows=pl.ds(0, HALF)):
        block = series_ref.at[tile, rows]
        for step in range(1, LAG_PARTS):
            copy(block, block, number, lag=(lag + step) % LAG_PARTS).start()

    def place_part(part):
        wait_all(others[part], 1 + part)
        placed = select_rows(
            placing,
            jnp.concatenate([arrived[:, 2 * part + slot, :] for slot in range(2)], axis=0),
        )
        theirs[part] = placed[HALF:]

        def start_swaps():
            for at, (piece_part, _) in enumerate(pieces):
                if piece_part == part:
                    swaps[at].start()

        if part == 0:

            @pl.when(segment == 0)
            def _():
                pl.semaphore_wait(late_sem, Z)

            start_swaps()
        else:
            pl.when(segment == 1)(start_swaps)

        series_ref[own_tile + part] = placed[:HALF]
        forward(own_tile + part, 11 + part)

    place_part(0)
    place_part(1)

    @pl.when(segment == 0)
    def _():
        send_sums_over()

    lag_tiles = pl.ds(lag * PARTS, PARTS)
    group_rows = pl.ds(pl.multiple_of((core * Y + y) * Z, Z), Z)

    def send_group(at, number):
        for low in range(NEAR):
            total = sums[at * Z + low, kept]
            for high in range(1, Z // NEAR):
                total = total + sums[at * Z + high * NEAR + low, kept]
            rows = pl.ds((core * Y + y) * Z + low * KEPT, KEPT)
            for part in range(PARTS):
                panel_ref[at, lag * PARTS + part, rows, :] = total[
                    part * KEPT : (part + 1) * KEPT
                ]
        group_tiles = panel_ref.at[at, lag_tiles, group_rows]
        for y_step in range(Y):
            for step in range(LAG_PARTS):
                if y_step or step:
                    copy(
                        group_tiles,
                        group_tiles,
                        number,
                        chan=owner((y + y_step) % Y, z, core),
                        lag=(lag + step) % LAG_PARTS,
                    ).start()

    seven_sums = sums.at[pl.ds(0, Z - 1), kept]
    eight_sums = sums.at[pl.ds(0, Z), kept]
    wait_all(seven_sums, 3)
    send_group(segment, 7)
    wait_all(eight_sums, 15)
    send_group(1 - segment, 16)

    for at, (part, rows) in enumerate(pieces):
        swaps[at].wait_recv()
        forward(other_tile + part, 17 + len(pieces) + at, rows)
        if at == HELD:

            @pl.when(segment == 0)
            def _():
                for swap in swaps[PIECES:]:
                    swap.start()

    xy_tiles = panel_ref.at[0, pl.ds(0, 5), pl.ds(0, 6 * Z)]
    wait_all(xy_tiles, 7)
    wait_all(xy_tiles, 16)
    core_rows = pl.ds(pl.multiple_of(core * Y * Z, Y * Z), Y * Z)
    half_panel = panel_ref.at[:, :, core_rows]
    across = copy(half_panel, half_panel, 8, chan=owner(y, z, 1 - core))
    across.start()
    three = series_ref.at[pl.ds(0, LAG_PARTS - 1)]
    for number in (11, 12):
        wait_all(three, number)
    three_pieces = series_ref.at[pl.ds(0, LAG_PARTS - 1), pl.ds(0, HALF // PIECES)]
    for at in range(len(pieces)):
        wait_all(three_pieces, 17 + len(pieces) + at)
    across.wait()
    wait_sent(near_others, 0)
    wait_sent(seven_sums, 3)
    wait_sent(eight_sums, 15)
    for part in range(PARTS):
        wait_sent(others[part], 1 + part)
    wait_sent(xy_tiles, 7)
    wait_sent(xy_tiles, 16)
    for number in (11, 12):
        wait_sent(three, number)
    for at in range(len(pieces)):
        wait_sent(three_pieces, 17 + len(pieces) + at)
    for swap in swaps:
        swap.wait_send()


def correlate(series_ref, panel_ref, out_ref, windows, shifts_high, shifts_low):
    lag_width = LAGS // LAG_PARTS
    rows = series_ref.shape[1]
    groups = lag_width // COLUMN_LAGS
    start = lax.axis_index("lag") * lag_width
    per_segment = TILES // SEGMENTS
    panel = jnp.concatenate(
        [panel_ref[tile // per_segment, tile % per_segment] for tile in range(TERMS // LANES)]
        + [jnp.zeros((REF, LANES), jnp.float32)] * (TILES - TERMS // LANES),
        axis=1,
    )
    panel = pltpu.roll(panel, start, 1)
    for shift in range(COLUMN_LAGS):
        high, low = split(pltpu.roll(panel, shift, 1) if shift else panel)
        shifts_high[pl.ds(shift * REF, REF), :] = high
        shifts_low[pl.ds(shift * REF, REF), :] = low
    series = jnp.concatenate([series_ref[tile] for tile in range(TILES)], axis=1)
    for group in range(groups):
        lag = group * COLUMN_LAGS
        high, low = split(pltpu.roll(series, SAMPLES - lag, 1) if lag else series)
        windows[pl.ds(group * rows, rows), :] = high
        windows[pl.ds((groups + group) * rows, rows), :] = low
    both = transposed_dot(windows[...], shifts_high[...])
    total = (
        both[: groups * rows]
        + transposed_dot(windows[pl.ds(0, groups * rows), :], shifts_low[...])
        + both[groups * rows :]
    )
    width = COLUMN_LAGS * REF
    for group in range(groups):
        out_ref[:, pl.ds(group * width, width)] = total[group * rows : (group + 1) * rows] * (
            1.0 / math.sqrt(TERMS)
        )


VMEM = pl.BlockSpec(memory_space=pltpu.VMEM)


def shards(records_owned, section_list, ref_index):
    series, panel = pl.pallas_call(
        exchange,
        out_shape=[
            jax.ShapeDtypeStruct((TILES, HALF, LANES), jnp.float32),
            jax.ShapeDtypeStruct((SEGMENTS, TILES // SEGMENTS, REF, LANES), jnp.float32),
        ],
        in_specs=[pl.BlockSpec(memory_space=pltpu.HBM)] * 3,
        out_specs=[VMEM] * 2,
        scratch_shapes=[
            pltpu.VMEM((ROWS * PARTS, LANES), jnp.float32),
            pltpu.VMEM((OWNERS, ROWS), jnp.int32),
            pltpu.VMEM((1, REF), jnp.int32),
            pltpu.VMEM((WIDE * NEAR, 8, LANES), jnp.float32),
            pltpu.VMEM((WIDE * NEAR, 8, LANES), jnp.float32),
            pltpu.VMEM((OWNERS, 8, LANES), jnp.float32),
            pltpu.VMEM((OWNERS, 8, LANES), jnp.float32),
            pltpu.VMEM((SEGMENTS * Z, 8, LANES), jnp.float32),
            pltpu.VMEM((PARTS, HALF, LANES), jnp.float32),
            pltpu.SemaphoreType.REGULAR,
            pltpu.SemaphoreType.DMA((3,)),
            pltpu.SemaphoreType.DMA((25,)),
            pltpu.SemaphoreType.DMA((25,)),
        ],
        compiler_params=pltpu.CompilerParams(
            collective_id=0, has_side_effects=True, vmem_limit_bytes=32 * 1024 * 1024
        ),
        name="exchange",
    )(
        *[
            pltpu.with_memory_space_constraint(value, pltpu.HBM)
            for value in (
                records_owned.reshape(ROWS * PARTS, LANES),
                section_list.reshape(OWNERS, ROWS),
                ref_index.reshape(1, REF),
            )
        ]
    )
    lag_width = LAGS // LAG_PARTS
    groups = lag_width // COLUMN_LAGS
    return pl.pallas_call(
        correlate,
        out_shape=jax.ShapeDtypeStruct((HALF, lag_width * REF), jnp.float32),
        in_specs=[VMEM] * 2,
        out_specs=VMEM,
        scratch_shapes=[pltpu.VMEM((2 * groups * HALF, SAMPLES), jnp.bfloat16)]
        + [pltpu.VMEM((COLUMN_LAGS * REF, SAMPLES), jnp.bfloat16)] * 2,
        compiler_params=pltpu.CompilerParams(vmem_limit_bytes=32 * 1024 * 1024),
        name="correlate",
    )(series, panel)


def solution(mesh):
    return jax.shard_map(
        shards,
        mesh=mesh,
        in_specs=(P("chan", "seg", "lag"), P(), P()),
        out_specs=P(("chan", "seg"), "lag"),
        check_vma=False,
    )
```
